32 devices in a mesh: user: 8 (over y, x, core), item: 4 (over z).
Axes of the slice: x: 2, y: 2, z: 4, core: 2. Of those that a mesh axis runs over, the one named last changes fastest.
Arguments:
- tokens: bfloat16 [16384, 1024], P(('user', 'item')), may hold values from -6 to 6
- lengths: int32 [32, 8], P(('user', 'item')), may hold values from 1 to 64, as said below
- destination: int32 [32, 8], P(('user', 'item')), may hold values from 0 to 7, as said below
- worker_offset: int32 [32, 8], P(('user', 'item')), may hold values from 0 to 255
- positives: int32 [16384], P(('user', 'item')), may hold values from 0 to 1023, as said below
- negatives: int32 [4, 256], replicated, may hold values from 0 to 1023, as said below
- table: bfloat16 [1024, 1024], P('item'), may hold values from -6 to 6
- in_gain: float32 [1024], replicated, may hold values from 0.1 to 1.9
- w_uvqk: bfloat16 [1024, 2048], P('item'), may hold values from -0.1875 to 0.1875
- out_gain: float32 [512], replicated, may hold values from 0.1 to 1.9
- w_out: bfloat16 [512, 1024], P(None, 'item'), may hold values from -0.25 to 0.25
Outputs:
- layer_out: bfloat16 [8192, 1024], P(('user', 'item'))
- token_grad: bfloat16 [16384, 1024], P(('user', 'item'))
- item_grad: float32 [1024, 1024], P('item', 'user')
The draws below stay inside these ranges and needn't reach their ends.
Inputs may be any that keep to these rules, and one draw needn't show every extreme that they name: `lengths`: A device's histories lie in its rows in order from row 0 and fill at most 512 rows; every destination receives a history of exactly 64 tokens. `destination`: A device sends its 8 histories to 8 different destinations along user; the histories sent to one device by the devices of its item index, placed at their worker_offset, cover its 256 rows exactly once. `positives`: the target ids of a device lie among the 256 table rows of its item index. `negatives`: columns k * 64 to k * 64 + 63 of each group name rows held by item index k.
All inputs are finite; a program needn't handle non-finite values.
Results may differ from the reference program's by a relative error of at most 0.017.
Values may be sent and summed in bfloat16 or wider, within the bound.
A program may use at most 64 MiB of HBM per device.

```python
import jax
import jax.numpy as jnp
from jax import lax

D = 1024
HEAD = 128
TOK_DEV = 256
HIST_DEV = 8
ITEM_DEV = 256
NEG = 256
HD = 512
MOST = 64
HOME = 512
ITEMS = 1024
NEG_SH = 64
N_USER = 8
N_ITEM = 4


def plan_tables(key):
    columns_count = N_ITEM
    users_count = N_USER
    hist_count = HIST_DEV
    longest = MOST
    total_rows = columns_count * users_count
    base_key = jax.random.fold_in(key, 9001)
    streams = jax.random.split(base_key, 6)
    slot = jnp.arange(hist_count, dtype=jnp.int32)
    opening = jnp.where(slot == 0, longest, 1).astype(jnp.int32)
    sizes_now = jnp.broadcast_to(opening, (total_rows, hist_count)).astype(jnp.int32)
    prefer = jax.random.randint(streams[0], (total_rows, hist_count), 1, 9).astype(jnp.int32)
    spare = TOK_DEV - longest - (hist_count - 1)

    def grow(step, current):
        raw = jax.random.randint(jax.random.fold_in(streams[1], step), (total_rows, hist_count), 0, 4096).astype(jnp.int32)
        ranked = raw * prefer * hist_count + slot[None, :]
        room = (current < longest - 1) & (slot[None, :] > 0)
        ranked = jnp.where(room, ranked, -1)
        chosen = jnp.argmax(ranked, axis=1).astype(jnp.int32)
        return current + (slot[None, :] == chosen[:, None]).astype(jnp.int32)
    sizes_now = lax.fori_loop(0, spare, grow, sizes_now)
    shuffle = jax.random.randint(streams[2], (total_rows, hist_count), 0, 4096).astype(jnp.int32) * hist_count + slot[None, :]
    order = jnp.argsort(shuffle, axis=1, stable=True)
    composed = jnp.take_along_axis(sizes_now, order, axis=1).reshape(columns_count, users_count, hist_count)

    def permutations(stream):
        keys_list = jax.random.split(stream, columns_count)
        return jax.vmap(lambda single: jax.random.permutation(single, users_count))(keys_list).astype(jnp.int32)
    alpha = permutations(streams[3])
    outer = permutations(streams[4])
    shifts = permutations(streams[5])[:, :hist_count]
    moved = (alpha[:, :, None] + shifts[:, None, :]) % users_count
    target = jnp.take_along_axis(outer, moved.reshape(columns_count, -1), axis=1).reshape(columns_count, users_count, hist_count)
    history_len = jnp.take_along_axis(composed, target, axis=1)
    starts = jnp.cumsum(composed, axis=2) - composed
    landing = jnp.take_along_axis(starts, target, axis=1)

    def layout(values):
        return jnp.transpose(values, (1, 0, 2)).reshape(users_count * columns_count, hist_count).astype(jnp.int32)
    return (layout(history_len), layout(target), layout(landing))


def draw_lengths(key, part):
    return plan_tables(key)[0]


def draw_destination(key, part):
    return plan_tables(key)[1]


def draw_worker_offset(key, part):
    return plan_tables(key)[2]


def draw_positives(key, part):
    total_rows = N_USER * N_ITEM * HOME
    item_of = jnp.arange(total_rows, dtype=jnp.int32) // HOME % N_ITEM
    chosen = jax.random.randint(jax.random.fold_in(key, 77), (total_rows,), 0, ITEM_DEV).astype(jnp.int32)
    return (item_of * ITEM_DEV + chosen).astype(jnp.int32)


def draw_negatives(key, part):
    block = (jnp.arange(NEG, dtype=jnp.int32) // NEG_SH).astype(jnp.int32)
    chosen = jax.random.randint(jax.random.fold_in(key, 55), (N_ITEM, NEG), 0, ITEM_DEV).astype(jnp.int32)
    return (block[None, :] * ITEM_DEV + chosen).astype(jnp.int32)


def block_levels(stream_key, extent, cuts, least, high):
    level, own = 1.0, jax.random.fold_in(stream_key, 6)
    for axis_at, shards_of in cuts:
        steps = jnp.exp(jax.random.uniform(jax.random.fold_in(own, axis_at), (shards_of,), jnp.float32, least / len(cuts), high / len(cuts)))
        level = level * jnp.repeat(steps, extent[axis_at] // shards_of).reshape([-1 if axis == axis_at else 1 for axis in range(len(extent))])
    return level


def gaussian(key, dims, scale, most, cuts=(), kind=jnp.bfloat16):
    loudness = block_levels(key, dims, cuts, -0.22, 0.18) if cuts else 1.0
    result = jax.random.normal(key, dims, jnp.float32) * scale * loudness
    return jnp.minimum(jnp.maximum(result, -most), most).astype(kind)


def setup_inputs(seed: int = 0) -> dict:
    seeds = jax.random.split(jax.random.key(seed), 12)
    return {
        "tokens": gaussian(seeds[0], (N_USER * N_ITEM * HOME, D), 1.0, 6.0, ((0, 32),)),
        "lengths": draw_lengths(jax.random.fold_in(seeds[11], 71), 0),
        "destination": draw_destination(jax.random.fold_in(seeds[11], 71), 0),
        "worker_offset": draw_worker_offset(jax.random.fold_in(seeds[11], 71), 0),
        "positives": draw_positives(jax.random.fold_in(seeds[11], 71), 0),
        "negatives": draw_negatives(jax.random.fold_in(seeds[11], 71), 0),
        "table": gaussian(seeds[6], (ITEMS, D), 1.0, 6.0, ((0, 4),)),
        "in_gain": jnp.clip(1.0 + 0.18 * jax.random.normal(seeds[7], (D,), jnp.float32), 0.1, 1.9),
        "w_uvqk": gaussian(seeds[8], (D, 4 * HD), D ** -0.5, 0.1875, ((0, 4),)),
        "out_gain": jnp.clip(1.0 + 0.18 * jax.random.normal(seeds[9], (HD,), jnp.float32), 0.1, 1.9),
        "w_out": gaussian(seeds[10], (HD, D), HD ** -0.5, 0.25, ((1, 4),)),
    }


norm_epsilon = 1e-05
scale_epsilon = 1e-06
inverse_temp = 20.0
loss_scale = 32.0

def layer_norm(values, gain):
    center = lax.optimization_barrier(jnp.mean(values, axis=-1, keepdims=True))
    shifted = values - center
    spread = lax.optimization_barrier(jnp.mean(shifted * shifted, axis=-1, keepdims=True))
    return shifted * lax.rsqrt(spread + norm_epsilon) * gain

def hstu_block(rows, segment, in_gain, w_uvqk, out_gain, w_out):
    count = rows.shape[0]
    rows_f = rows.astype(jnp.float32)
    normed = layer_norm(rows_f, in_gain).astype(jnp.bfloat16)
    active = jax.nn.silu(jnp.dot(normed, w_uvqk, preferred_element_type=jnp.float32)).astype(jnp.bfloat16)
    width = active.shape[1] // 4
    heads = width // HEAD

    def split_heads(block):
        return block.reshape(count, heads, HEAD).astype(jnp.float32)
    gate_u = active[:, :width]
    values_v = split_heads(active[:, width:2 * width])
    queries = split_heads(active[:, 2 * width:3 * width])
    key_rows = split_heads(active[:, 3 * width:])
    scores = jnp.einsum('qhd,khd->hqk', queries, key_rows) * HEAD ** (-0.5)
    order = jnp.arange(count, dtype=jnp.int32)
    allowed = (segment[:, None] == segment[None, :]) & (order[None, :] <= order[:, None])
    weights = jnp.where(allowed[None], jax.nn.silu(scores), 0.0).astype(jnp.bfloat16)
    mixed = jnp.einsum('hqk,khd->qhd', weights.astype(jnp.float32), values_v).reshape(count, width)
    gated = (layer_norm(mixed, out_gain) * gate_u.astype(jnp.float32)).astype(jnp.bfloat16)
    return (rows_f + jnp.dot(gated, w_out, preferred_element_type=jnp.float32)).astype(jnp.bfloat16)

def reference(tokens, lengths, destination, worker_offset, positives, negatives, table, in_gain, w_uvqk, out_gain, w_out):
    devices = N_USER * N_ITEM
    history_len = lengths.astype(jnp.int32)
    home_start = (jnp.cumsum(history_len, axis=1) - history_len).astype(jnp.int32)
    ends = (home_start + history_len).astype(jnp.int32)
    row_ids = jnp.arange(HOME, dtype=jnp.int32)
    segment = lax.optimization_barrier(jnp.sum((row_ids[None, :, None] >= ends[:, None, :]).astype(jnp.int32), axis=2)).astype(jnp.int32)
    valid = row_ids[None, :] < lax.optimization_barrier(jnp.sum(history_len, axis=1)).astype(jnp.int32)[:, None]
    history = jnp.minimum(segment, HIST_DEV - 1).astype(jnp.int32)
    item_of = (jnp.arange(devices, dtype=jnp.int32) % N_ITEM).astype(jnp.int32)
    worker_dev = (destination.astype(jnp.int32) * N_ITEM + item_of[:, None]).astype(jnp.int32)

    def pick(values):
        return jnp.take_along_axis(values, history, axis=1).astype(jnp.int32)
    target = pick(worker_dev) * TOK_DEV + pick(worker_offset.astype(jnp.int32)) + row_ids[None, :] - pick(home_start)
    target = jnp.where(valid, target, devices * TOK_DEV).reshape(-1).astype(jnp.int32)
    home_index = jnp.arange(devices * HOME, dtype=jnp.int32)
    source = jnp.zeros((devices * TOK_DEV,), jnp.int32).at[target].set(home_index, mode='drop')
    worker_input = tokens[source].reshape(devices, TOK_DEV, D)
    worker_segment = (source // HOME).astype(jnp.int32).reshape(devices, TOK_DEV)
    computed = lax.map(lambda pair: hstu_block(pair[0], pair[1], in_gain, w_uvqk, out_gain, w_out), (worker_input, worker_segment))
    layer_out = computed.reshape(devices * TOK_DEV, D)
    flat_valid = valid.reshape(-1)
    clipped = jnp.minimum(target, devices * TOK_DEV - 1).astype(jnp.int32)
    home_out = jnp.where(flat_valid[:, None], layer_out[clipped], jnp.zeros((), layer_out.dtype))
    table_f = table.astype(jnp.float32)
    table_scale = lax.rsqrt(lax.optimization_barrier(jnp.mean(table_f * table_f, axis=1)) + scale_epsilon)
    table_hat = table_f * table_scale[:, None]
    table_low = table_hat.astype(jnp.bfloat16)

    def by_column(values):
        shaped = values.reshape((N_USER, N_ITEM, HOME) + values.shape[1:])
        moved = jnp.moveaxis(shaped, 1, 0)
        return moved.reshape((N_ITEM, N_USER * HOME) + values.shape[1:])
    out_cols = by_column(home_out)
    valid_cols = by_column(flat_valid)
    positive_cols = by_column(positives.astype(jnp.int32))
    negative_rows = table_low[negatives.astype(jnp.int32)]
    factor = inverse_temp / D

    def column(inputs):
        out_rows, valid_rows, positive_ids, group_rows, column_index = inputs
        out_f = out_rows.astype(jnp.float32)
        out_scale = lax.rsqrt(lax.optimization_barrier(jnp.mean(out_f * out_f, axis=1)) + scale_epsilon)
        out_hat = out_f * out_scale[:, None]
        out_low = out_hat.astype(jnp.bfloat16)
        positive_rows = table_low[positive_ids]
        positive_logit = lax.optimization_barrier(jnp.sum(out_low.astype(jnp.float32) * positive_rows.astype(jnp.float32), axis=1)) * factor
        negative_logit = jnp.dot(out_low, group_rows.T, preferred_element_type=jnp.float32) * factor
        positive_exp = jnp.exp(positive_logit)
        negative_exp = jnp.exp(negative_logit)
        partition = positive_exp + lax.optimization_barrier(jnp.sum(negative_exp, axis=1))
        weight = jnp.where(valid_rows, loss_scale, 0.0)
        positive_grad = weight * (positive_exp / partition - 1.0)
        negative_grad = (weight[:, None] * negative_exp / partition[:, None]).astype(jnp.bfloat16)
        grad_hat = (positive_grad[:, None] * positive_rows.astype(jnp.float32) + jnp.dot(negative_grad, group_rows, preferred_element_type=jnp.float32)) * factor
        token_part = ((grad_hat - out_hat * lax.optimization_barrier(jnp.mean(grad_hat * out_hat, axis=1, keepdims=True))) * out_scale[:, None]).astype(jnp.bfloat16)
        negative_terms = jnp.dot(negative_grad.T, out_low, preferred_element_type=jnp.float32) * factor
        local_ids = (positive_ids - column_index * ITEM_DEV).astype(jnp.int32)
        positive_terms = jax.ops.segment_sum((positive_grad * factor)[:, None] * out_low.astype(jnp.float32), local_ids, num_segments=ITEM_DEV)
        return (token_part, negative_terms, positive_terms)
    token_cols, negative_terms, positive_terms = lax.map(column, (out_cols, valid_cols, positive_cols, negative_rows, jnp.arange(N_ITEM, dtype=jnp.int32)))
    token_grad = jnp.moveaxis(token_cols.reshape(N_ITEM, N_USER, HOME, D), 0, 1).reshape(devices * HOME, D)
    row_sums = positive_terms.reshape(ITEMS, D) + jnp.zeros((ITEMS, D), jnp.float32).at[negatives.reshape(-1).astype(jnp.int32)].add(negative_terms.reshape(-1, D))
    item_grad = (row_sums - table_hat * lax.optimization_barrier(jnp.mean(row_sums * table_hat, axis=1, keepdims=True))) * table_scale[:, None]
    return (layer_out, token_grad, item_grad)
```

```python
import functools

import jax
import jax.numpy as jnp
from jax import lax
from jax.experimental import pallas as pl
from jax.experimental.pallas import tpu as pltpu
from jax.sharding import PartitionSpec as P

HEAD = 128
TOK_DEV = 256


norm_epsilon = 1e-05
scale_epsilon = 1e-06
inverse_temp = 20.0
loss_scale = 32.0


def layer_norm(values, gain):
    center = jnp.mean(values, axis=-1, keepdims=True)
    shifted = values - center
    spread = jnp.mean(shifted * shifted, axis=-1, keepdims=True)
    return shifted * lax.rsqrt(spread + norm_epsilon) * gain


def hstu_block(rows, segment, in_gain, w_uvqk, out_gain, w_out):
    count = rows.shape[0]
    rows_f = rows.astype(jnp.float32)
    normed = layer_norm(rows_f, in_gain).astype(jnp.bfloat16)
    projected = jnp.dot(
        normed,
        lax.all_gather(w_uvqk, "item", axis=0, tiled=True),
        preferred_element_type=jnp.float32,
    )
    active = jax.nn.silu(projected).astype(jnp.bfloat16)
    width = active.shape[1] // 4
    heads = width // HEAD
    gate_u = active[:, :width]
    values_v = active[:, width : 2 * width].reshape(count, heads, HEAD)
    queries = active[:, 2 * width : 3 * width].reshape(count, heads, HEAD)
    key_rows = active[:, 3 * width :].reshape(count, heads, HEAD)
    scores = jnp.einsum(
        "qhd,khd->hqk", queries, key_rows, preferred_element_type=jnp.float32
    ) * HEAD ** (-0.5)
    order = jnp.arange(count, dtype=jnp.int32)
    allowed = (segment[:, None] == segment[None, :]) & (order[None, :] <= order[:, None])
    weights = jnp.where(allowed[None], jax.nn.silu(scores), 0.0).astype(jnp.bfloat16)
    mixed = jnp.einsum(
        "hqk,khd->qhd", weights, values_v, preferred_element_type=jnp.float32
    ).reshape(count, width)
    gated = (layer_norm(mixed, out_gain) * gate_u.astype(jnp.float32)).astype(jnp.bfloat16)
    delta = jnp.dot(
        gated, lax.all_gather(w_out, "item", axis=1, tiled=True), preferred_element_type=jnp.float32
    )
    return (rows_f + delta).astype(jnp.bfloat16)


def dispatch(rows, home_start, history_len, targets, offsets, slot_rows, user_count):
    peers = jnp.arange(user_count, dtype=jnp.int32)
    chosen = (targets[None, :] == peers[:, None]).astype(jnp.int32)
    first_row = jnp.sum(chosen * home_start[None, :], axis=1)
    sent_count = jnp.sum(chosen * history_len[None, :], axis=1)
    landing = jnp.sum(chosen * offsets[None, :], axis=1)
    within = jnp.arange(slot_rows, dtype=jnp.int32)
    picked = jnp.minimum(first_row[:, None] + within[None, :], rows.shape[0] - 1)
    filled = within[None, :] < sent_count[:, None]
    parcels = jnp.where(filled[:, :, None], rows[picked], jnp.zeros((), rows.dtype))
    labels = jnp.stack([landing, sent_count], axis=1)
    arrived, arrived_labels = (
        lax.all_to_all(parcels, "user", split_axis=0, concat_axis=0, tiled=True),
        lax.all_to_all(labels, "user", split_axis=0, concat_axis=0, tiled=True),
    )
    worker_rows = jnp.arange(TOK_DEV, dtype=jnp.int32)
    lower = arrived_labels[:, 0]
    upper = lower + arrived_labels[:, 1]
    inside = (
        (worker_rows[:, None] >= lower[None, :]) & (worker_rows[:, None] < upper[None, :])
    ).astype(jnp.int32)
    source = jnp.sum(inside * peers[None, :], axis=1)
    begin = jnp.sum(inside * lower[None, :], axis=1)
    flattened = arrived.reshape(-1, arrived.shape[-1])
    gathered = flattened[source * slot_rows + worker_rows - begin]
    return (gathered, source, arrived_labels)


def per_device(
    tokens,
    lengths,
    destination,
    worker_offset,
    positives,
    negatives,
    table,
    in_gain,
    w_uvqk,
    out_gain,
    w_out,
):
    user_count = lax.axis_size("user")
    item_count = lax.axis_size("item")
    item_here = lax.axis_index("item")
    user_here = lax.axis_index("user")
    home_rows = tokens.shape[0]
    model_width = tokens.shape[1]
    hist_count = lengths.shape[1]
    slot_rows = home_rows // hist_count
    history_len = lengths[0]
    targets = destination[0]
    offsets = worker_offset[0]
    home_start = jnp.cumsum(history_len) - history_len
    row_ids = jnp.arange(home_rows, dtype=jnp.int32)
    finished = (row_ids[:, None] >= (home_start + history_len)[None, :]).astype(jnp.int32)
    home_segment = jnp.sum(finished, axis=1)
    valid = row_ids < jnp.sum(history_len)
    home_out = hstu_block(tokens, home_segment, in_gain, w_uvqk, out_gain, w_out)
    layer_out = dispatch(
        home_out, home_start, history_len, targets, offsets, slot_rows, user_count
    )[0]
    item_rows = table.shape[0]
    table_f = table.astype(jnp.float32)
    table_scale = lax.rsqrt(jnp.mean(table_f * table_f, axis=1) + scale_epsilon)
    table_hat = table_f * table_scale[:, None]
    table_low = table_hat.astype(jnp.bfloat16)
    share = negatives.shape[1] // item_count
    owned_ids = (
        lax.dynamic_slice_in_dim(negatives, item_here * share, share, 1) - item_here * item_rows
    )
    group_rows = lax.all_to_all(
        table_low[owned_ids], "item", split_axis=0, concat_axis=0, tiled=True
    ).reshape(-1, model_width)
    positive_local = positives - item_here * item_rows
    positive_rows = table_low[positive_local]
    out_f = home_out.astype(jnp.float32)
    out_scale = lax.rsqrt(jnp.mean(out_f * out_f, axis=1) + scale_epsilon)
    out_hat = out_f * out_scale[:, None]
    out_low = out_hat.astype(jnp.bfloat16)
    factor = inverse_temp / model_width
    positive_logit = (
        jnp.einsum("rd,rd->r", out_low, positive_rows, preferred_element_type=jnp.float32) * factor
    )
    negative_logit = (
        jnp.einsum("rd,nd->rn", out_low, group_rows, preferred_element_type=jnp.float32) * factor
    )
    positive_exp = jnp.exp(positive_logit)
    negative_exp = jnp.exp(negative_logit)
    partition = positive_exp + jnp.sum(negative_exp, axis=1)
    weight = jnp.where(valid, loss_scale, 0.0)
    positive_grad = weight * (positive_exp / partition - 1.0)
    negative_grad = (weight[:, None] * negative_exp / partition[:, None]).astype(jnp.bfloat16)
    grad_hat = (
        positive_grad[:, None] * positive_rows.astype(jnp.float32)
        + jnp.dot(negative_grad, group_rows, preferred_element_type=jnp.float32)
    ) * factor
    token_grad = (
        (grad_hat - out_hat * jnp.mean(grad_hat * out_hat, axis=1, keepdims=True))
        * out_scale[:, None]
    ).astype(jnp.bfloat16)
    negative_terms = (
        jnp.einsum("rn,rd->nd", negative_grad, out_low, preferred_element_type=jnp.float32) * factor
    )
    owned_terms = lax.all_to_all(
        negative_terms.reshape(item_count, share, model_width).astype(jnp.bfloat16),
        "item",
        split_axis=0,
        concat_axis=0,
        tiled=True,
    ).astype(jnp.float32)
    positive_terms = (positive_grad * factor)[:, None] * out_low.astype(jnp.float32)
    catalog = jnp.arange(item_rows, dtype=jnp.int32)
    positive_hits = (positive_local[None, :] == catalog[:, None]).astype(jnp.float32)
    negative_hits = (owned_ids.reshape(-1)[None, :] == catalog[:, None]).astype(jnp.float32)
    row_sums = jnp.dot(positive_hits, positive_terms, precision=lax.Precision.HIGHEST)
    row_sums = row_sums + jnp.dot(
        negative_hits, owned_terms.reshape(-1, model_width), precision=lax.Precision.HIGHEST
    )
    column_width = model_width // user_count
    totals = lax.psum(row_sums.astype(jnp.bfloat16), "user").astype(jnp.float32)
    inner = jnp.mean(totals * table_hat, axis=1)
    whole = (totals - table_hat * inner[:, None]) * table_scale[:, None]
    item_grad = lax.dynamic_slice_in_dim(whole, user_here * column_width, column_width, 1)
    return (layer_out, token_grad, item_grad)


MESH = pl.DeviceIdType.MESH
VMEM_SPEC = pl.BlockSpec(memory_space=pltpu.VMEM)


def remote(src, dst, send_sem, recv_sem, user, item):
    return pltpu.make_async_remote_copy(
        src_ref=src,
        dst_ref=dst,
        send_sem=send_sem,
        recv_sem=recv_sem,
        device_id=(user, item),
        device_id_type=MESH,
    )


def greet(users, items, u, i):
    barrier = pltpu.get_barrier_semaphore()
    for d in range(1, users):
        pl.semaphore_signal(
            barrier, inc=1, device_id=(lax.rem(u + d, users), i), device_id_type=MESH
        )
    for d in range(1, items):
        pl.semaphore_signal(
            barrier, inc=1, device_id=(u, lax.rem(i + d, items)), device_id_type=MESH
        )
    pl.semaphore_wait(barrier, users + items - 2)


def gather_kernel(
    users, items, w_ref, o_ref, n_ref, l_ref, wf, of, nf, lf,
    own_sem, s1, r1, s2, r2, s3, r3, sn, rn, sl, rl,
):
    u = lax.axis_index("user")
    i = lax.axis_index("item")
    sibling = u + 1 - 2 * lax.rem(u, 2)
    half = users // 2
    greet(users, items, u, i)
    pairs = ((w_ref, wf), (o_ref, of))
    sent = []
    for a, (src, dst) in enumerate(pairs):
        for d in range(1, items):
            c = remote(src.at[u], dst.at[i, u], s1.at[a, d - 1], r1.at[a, d - 1], u, lax.rem(i + d, items))
            c.start()
            sent.append(c)
    for d in range(1, users):
        u2 = lax.rem(u + d, users)
        c = remote(l_ref.at[u2], lf.at[u], sl.at[d - 1], rl.at[d - 1], u2, i)
        c.start()
        sent.append(c)
    for d in range(1, items):
        i2 = lax.rem(i + d, items)
        c = remote(n_ref.at[i2], nf.at[i], sn.at[d - 1], rn.at[d - 1], u, i2)
        c.start()
        sent.append(c)
    local = [
        pltpu.make_async_copy(w_ref, wf.at[i], own_sem.at[0]),
        pltpu.make_async_copy(o_ref, of.at[i], own_sem.at[1]),
        pltpu.make_async_copy(n_ref.at[i], nf.at[i], own_sem.at[2]),
        pltpu.make_async_copy(l_ref.at[u], lf.at[u], own_sem.at[3]),
    ]
    for c in local:
        c.start()
    for a, (src, dst) in enumerate(pairs):
        for d in range(1, items):
            i2 = lax.rem(i + items - d, items)
            piece = dst.at[i2, u]
            remote(piece, piece, s1.at[a, d - 1], r1.at[a, d - 1], u, i2).wait_recv()
            for e in range(1, half):
                c = remote(piece, piece, s2.at[a, d - 1, e - 1], r2.at[a, d - 1, e - 1], lax.rem(u + 2 * e, users), i)
                c.start()
                sent.append(c)
            c = remote(piece, piece, s3.at[a, d - 1, 0], r3.at[a, d - 1, 0], sibling, i)
            c.start()
            sent.append(c)
    for a, (src, dst) in enumerate(pairs):
        for d in range(1, items):
            i2 = lax.rem(i + items - d, items)
            for e in range(1, half):
                u2 = lax.rem(u + users - 2 * e, users)
                piece = dst.at[i2, u2]
                remote(piece, piece, s2.at[a, d - 1, e - 1], r2.at[a, d - 1, e - 1], u2, i).wait_recv()
                c = remote(piece, piece, s3.at[a, d - 1, e], r3.at[a, d - 1, e], sibling, i)
                c.start()
                sent.append(c)
    for a, (src, dst) in enumerate(pairs):
        for d in range(1, items):
            i2 = lax.rem(i + items - d, items)
            for e in range(half):
                piece = dst.at[i2, lax.rem(sibling + users - 2 * e, users)]
                remote(piece, piece, s3.at[a, d - 1, e], r3.at[a, d - 1, e], sibling, i).wait_recv()
    for d in range(1, items):
        i2 = lax.rem(i + items - d, items)
        remote(nf.at[i2], nf.at[i2], sn.at[d - 1], rn.at[d - 1], u, i2).wait_recv()
    for d in range(1, users):
        u2 = lax.rem(u + users - d, users)
        remote(lf.at[u2], lf.at[u2], sl.at[d - 1], rl.at[d - 1], u2, i).wait_recv()
    for c in local:
        c.wait()
    for c in sent:
        c.wait_send()


def gather_all(users, items, w, w_o, rows, labels):
    dma = pltpu.SemaphoreType.DMA
    half = users // 2
    w3 = w.reshape(users, w.shape[0] // users, w.shape[1])
    o3 = w_o.reshape(users, w_o.shape[0] // users, w_o.shape[1])
    return pl.pallas_call(
        functools.partial(gather_kernel, users, items),
        out_shape=(
            jax.ShapeDtypeStruct((items,) + w3.shape, w.dtype),
            jax.ShapeDtypeStruct((items,) + o3.shape, w_o.dtype),
            jax.ShapeDtypeStruct(rows.shape, rows.dtype),
            jax.ShapeDtypeStruct(labels.shape, labels.dtype),
        ),
        in_specs=[VMEM_SPEC] * 4,
        out_specs=(VMEM_SPEC,) * 4,
        scratch_shapes=[
            dma((4,)),
            dma((2, items - 1)), dma((2, items - 1)),
            dma((2, items - 1, half - 1)), dma((2, items - 1, half - 1)),
            dma((2, items - 1, half)), dma((2, items - 1, half)),
            dma((items - 1,)), dma((items - 1,)),
            dma((users - 1,)), dma((users - 1,)),
        ],
        compiler_params=pltpu.CompilerParams(collective_id=0, has_side_effects=True),
    )(w3, o3, rows, labels)


def tail_kernel(
    users, items, parcels, terms, pos_sums, neg_hits, place, table_hat, table_scale,
    layer_out, item_grad,
    arrived, owned, chunks, got, inner_out, inner_got,
    own_sem, sd, rd, sn, rn, sc, rc, si, ri,
):
    u = lax.axis_index("user")
    i = lax.axis_index("item")
    width = layer_out.shape[1]
    cols = width // users
    greet(users, items, u, i)
    sent = []
    for d in range(1, items):
        i2 = lax.rem(i + d, items)
        c = remote(terms.at[i2], owned.at[i], sn.at[d - 1], rn.at[d - 1], u, i2)
        c.start()
        sent.append(c)
    for d in range(1, users):
        u2 = lax.rem(u + d, users)
        c = remote(parcels.at[u2], arrived.at[u], sd.at[d - 1], rd.at[d - 1], u2, i)
        c.start()
        sent.append(c)
    local = [
        pltpu.make_async_copy(terms.at[i], owned.at[i], own_sem.at[0]),
        pltpu.make_async_copy(parcels.at[u], arrived.at[u], own_sem.at[1]),
    ]
    for c in local:
        c.start()
    for c in local:
        c.wait()
    for d in range(1, items):
        i2 = lax.rem(i + items - d, items)
        remote(owned.at[i2], owned.at[i2], sn.at[d - 1], rn.at[d - 1], u, i2).wait_recv()
    row_sums = pos_sums[...] + jnp.dot(
        neg_hits[...], owned[...].reshape(-1, width), preferred_element_type=jnp.float32
    )
    for v in range(users):
        chunks[v] = row_sums[:, v * cols : (v + 1) * cols].astype(jnp.bfloat16)
    inner = jnp.mean(row_sums * table_hat[...], axis=1, keepdims=True)
    inner_out[...] = jnp.transpose(jnp.broadcast_to(inner, (inner.shape[0], 128)))[:8]
    for d in range(1, users):
        u2 = lax.rem(u + d, users)
        c = remote(chunks.at[u2], got.at[u], sc.at[d - 1], rc.at[d - 1], u2, i)
        c.start()
        sent.append(c)
        c = remote(inner_out, inner_got.at[u], si.at[d - 1], ri.at[d - 1], u2, i)
        c.start()
        sent.append(c)
    total = chunks[u].astype(jnp.float32)
    inner_total = inner_out[...]
    for d in range(1, users):
        u2 = lax.rem(u + users - d, users)
        remote(arrived.at[u2], arrived.at[u2], sd.at[d - 1], rd.at[d - 1], u2, i).wait_recv()
    layer_out[...] = jnp.dot(
        place[...], arrived[...].reshape(-1, width), preferred_element_type=jnp.float32
    ).astype(jnp.bfloat16)
    for d in range(1, users):
        u2 = lax.rem(u + users - d, users)
        remote(got.at[u2], got.at[u2], sc.at[d - 1], rc.at[d - 1], u2, i).wait_recv()
        remote(inner_got.at[u2], inner_got.at[u2], si.at[d - 1], ri.at[d - 1], u2, i).wait_recv()
        total = total + got[u2].astype(jnp.float32)
        inner_total = inner_total + inner_got[u2]
    inner_rows = jnp.transpose(jnp.broadcast_to(inner_total[:1], (128, inner_total.shape[1])))
    here = table_hat[:, pl.ds(pl.multiple_of(u * cols, cols), cols)]
    item_grad[...] = (total - here * inner_rows[:, :cols]) * table_scale[...]
    for c in sent:
        c.wait_send()


def tail(users, items, parcels, terms, pos_sums, neg_hits, place, table_hat, table_scale):
    dma = pltpu.SemaphoreType.DMA
    width = parcels.shape[-1]
    cols = width // users
    count = table_hat.shape[0]
    return pl.pallas_call(
        functools.partial(tail_kernel, users, items),
        out_shape=(
            jax.ShapeDtypeStruct((place.shape[0], width), jnp.bfloat16),
            jax.ShapeDtypeStruct((count, cols), jnp.float32),
        ),
        in_specs=[VMEM_SPEC] * 7,
        out_specs=(VMEM_SPEC,) * 2,
        scratch_shapes=[
            pltpu.VMEM(parcels.shape, jnp.bfloat16),
            pltpu.VMEM(terms.shape, jnp.bfloat16),
            pltpu.VMEM((users, count, cols), jnp.bfloat16),
            pltpu.VMEM((users, count, cols), jnp.bfloat16),
            pltpu.VMEM((8, count), jnp.float32),
            pltpu.VMEM((users, 8, count), jnp.float32),
            dma((2,)),
            dma((users - 1,)), dma((users - 1,)),
            dma((items - 1,)), dma((items - 1,)),
            dma((users - 1,)), dma((users - 1,)),
            dma((users - 1,)), dma((users - 1,)),
        ],
        compiler_params=pltpu.CompilerParams(collective_id=1, has_side_effects=True),
    )(parcels, terms, pos_sums, neg_hits, place, table_hat, table_scale)


def hstu_whole(rows, segment, in_gain, w_full, out_gain, w_out_full):
    count = rows.shape[0]
    rows_f = rows.astype(jnp.float32)
    normed = layer_norm(rows_f, in_gain).astype(jnp.bfloat16)
    projected = jnp.dot(normed, w_full, preferred_element_type=jnp.float32)
    active = jax.nn.silu(projected).astype(jnp.bfloat16)
    width = active.shape[1] // 4
    heads = width // HEAD
    gate_u = active[:, :width]
    values_v = active[:, width : 2 * width].reshape(count, heads, HEAD)
    queries = active[:, 2 * width : 3 * width].reshape(count, heads, HEAD)
    key_rows = active[:, 3 * width :].reshape(count, heads, HEAD)
    scores = jnp.einsum(
        "qhd,khd->hqk", queries, key_rows, preferred_element_type=jnp.float32
    ) * HEAD ** (-0.5)
    order = jnp.arange(count, dtype=jnp.int32)
    allowed = (segment[:, None] == segment[None, :]) & (order[None, :] <= order[:, None])
    weights = jnp.where(allowed[None], jax.nn.silu(scores), 0.0).astype(jnp.bfloat16)
    mixed = jnp.einsum(
        "hqk,khd->qhd", weights, values_v, preferred_element_type=jnp.float32
    ).reshape(count, width)
    gated = (layer_norm(mixed, out_gain) * gate_u.astype(jnp.float32)).astype(jnp.bfloat16)
    delta = jnp.concatenate(
        [jnp.dot(gated, w_out_full[k], preferred_element_type=jnp.float32) for k in range(w_out_full.shape[0])],
        axis=1,
    )
    return (rows_f + delta).astype(jnp.bfloat16)


def per_device_kernels(
    users, items,
    tokens, lengths, destination, worker_offset, positives, negatives, table,
    in_gain, w_uvqk, out_gain, w_out,
):
    item_here = lax.axis_index("item")
    home_rows, model_width = tokens.shape
    slot_rows = home_rows // lengths.shape[1]
    history_len = lengths[0]
    targets = destination[0]
    offsets = worker_offset[0]
    upto = jnp.arange(lengths.shape[1], dtype=jnp.int32)
    home_start = jnp.sum(
        jnp.where(upto[None, :] < upto[:, None], history_len[None, :], 0), axis=1
    )
    row_ids = jnp.arange(home_rows, dtype=jnp.int32)
    finished = (row_ids[:, None] >= (home_start + history_len)[None, :]).astype(jnp.int32)
    home_segment = jnp.sum(finished, axis=1)
    valid = row_ids < jnp.sum(history_len)
    peers = jnp.arange(users, dtype=jnp.int32)
    chosen = (targets[None, :] == peers[:, None]).astype(jnp.int32)
    first_row = jnp.sum(chosen * home_start[None, :], axis=1)
    sent_count = jnp.sum(chosen * history_len[None, :], axis=1)
    landing = jnp.sum(chosen * offsets[None, :], axis=1)
    lane = jnp.arange(128, dtype=jnp.int32)
    labels = jnp.where(lane[None, :] == 0, landing[:, None], sent_count[:, None])
    labels = jnp.broadcast_to(labels[:, None, :], (users, 8, 128))
    item_rows = table.shape[0]
    table_f = table.astype(jnp.float32)
    table_scale = lax.rsqrt(jnp.mean(table_f * table_f, axis=1) + scale_epsilon)
    table_hat = table_f * table_scale[:, None]
    table_low = table_hat.astype(jnp.bfloat16)
    share = negatives.shape[1] // items
    owned_ids = (
        lax.dynamic_slice_in_dim(negatives, item_here * share, share, 1) - item_here * item_rows
    ).reshape(-1)
    catalog = jnp.arange(item_rows, dtype=jnp.int32)
    owned_pick = (owned_ids[:, None] == catalog[None, :]).astype(jnp.bfloat16)
    owned_rows = jnp.dot(owned_pick, table_low)
    w_full, w_out_full, group_rows, arrived_labels = gather_all(
        users, items, w_uvqk, w_out, owned_rows.reshape(items, share, model_width), labels
    )
    home_out = hstu_whole(
        tokens, home_segment, in_gain, w_full.reshape(-1, w_uvqk.shape[1]), out_gain,
        w_out_full.reshape(items, w_out.shape[0], w_out.shape[1]),
    )
    group_rows = group_rows.reshape(-1, model_width)
    within = jnp.arange(slot_rows, dtype=jnp.int32)
    wanted = jnp.where(
        within[None, :] < sent_count[:, None], first_row[:, None] + within[None, :], -1
    ).reshape(-1)
    parcel_pick = (wanted[:, None] == row_ids[None, :]).astype(jnp.bfloat16)
    parcels = jnp.dot(parcel_pick, home_out).reshape(users, slot_rows, model_width)
    lower = arrived_labels[:, 0, 0]
    counts = arrived_labels[:, 0, 1]
    landed = jnp.where(
        within[None, :] < counts[:, None], lower[:, None] + within[None, :], -1
    ).reshape(-1)
    worker_rows = jnp.arange(TOK_DEV, dtype=jnp.int32)
    place = (landed[None, :] == worker_rows[:, None]).astype(jnp.bfloat16)
    positive_local = positives - item_here * item_rows
    positive_pick = positive_local[:, None] == catalog[None, :]
    positive_rows = jnp.dot(positive_pick.astype(jnp.bfloat16), table_low)
    out_f = home_out.astype(jnp.float32)
    out_scale = lax.rsqrt(jnp.mean(out_f * out_f, axis=1) + scale_epsilon)
    out_hat = out_f * out_scale[:, None]
    out_low = out_hat.astype(jnp.bfloat16)
    factor = inverse_temp / model_width
    positive_logit = (
        jnp.sum(out_low.astype(jnp.float32) * positive_rows.astype(jnp.float32), axis=1) * factor
    )
    negative_logit = (
        jnp.einsum("rd,nd->rn", out_low, group_rows, preferred_element_type=jnp.float32) * factor
    )
    positive_exp = jnp.exp(positive_logit)
    negative_exp = jnp.exp(negative_logit)
    partition = positive_exp + jnp.sum(negative_exp, axis=1)
    weight = jnp.where(valid, loss_scale, 0.0)
    positive_grad = weight * (positive_exp / partition - 1.0)
    negative_grad = (weight[:, None] * negative_exp / partition[:, None]).astype(jnp.bfloat16)
    grad_hat = (
        positive_grad[:, None] * positive_rows.astype(jnp.float32)
        + jnp.dot(negative_grad, group_rows, preferred_element_type=jnp.float32)
    ) * factor
    token_grad = (
        (grad_hat - out_hat * jnp.mean(grad_hat * out_hat, axis=1, keepdims=True))
        * out_scale[:, None]
    ).astype(jnp.bfloat16)
    negative_terms = (
        jnp.einsum("rn,rd->nd", negative_grad, out_low, preferred_element_type=jnp.float32) * factor
    ).astype(jnp.bfloat16).reshape(items, share, model_width)
    pos_w = positive_grad * factor
    pos_hi = pos_w.astype(jnp.bfloat16)
    pos_lo = (pos_w - pos_hi.astype(jnp.float32)).astype(jnp.bfloat16)
    zero = jnp.zeros((), jnp.bfloat16)
    hits_hi = jnp.where(positive_pick, pos_hi[:, None], zero)
    hits_lo = jnp.where(positive_pick, pos_lo[:, None], zero)
    pos_sums = jnp.einsum(
        "rc,rd->cd", hits_hi, out_low, preferred_element_type=jnp.float32
    ) + jnp.einsum("rc,rd->cd", hits_lo, out_low, preferred_element_type=jnp.float32)
    neg_hits = (owned_ids[None, :] == catalog[:, None]).astype(jnp.bfloat16)
    layer_out, item_grad = tail(
        users, items, parcels, negative_terms, pos_sums, neg_hits, place, table_hat,
        table_scale[:, None],
    )
    return (layer_out, token_grad, item_grad)


def step(users, items, tokens, lengths, destination, worker_offset, positives, negatives, table,
         in_gain, w_uvqk, out_gain, w_out):
    aligned = (
        users % 2 == 0
        and users > 2
        and items > 1
        and w_uvqk.shape[0] % (16 * users) == 0
        and w_out.shape[0] % (16 * users) == 0
        and w_out.shape[1] % 128 == 0
        and tokens.shape[1] == 128 * users
        and table.shape[0] % 128 == 0
        and negatives.shape[1] % (16 * items) == 0
    )
    run = functools.partial(per_device_kernels, users, items) if aligned else per_device
    return run(tokens, lengths, destination, worker_offset, positives, negatives, table,
               in_gain, w_uvqk, out_gain, w_out)


def solution(mesh):
    return jax.shard_map(
        functools.partial(step, mesh.shape["user"], mesh.shape["item"]),
        mesh=mesh,
        in_specs=(
            P(("user", "item"), None),
            P(("user", "item"), None),
            P(("user", "item"), None),
            P(("user", "item"), None),
            P(("user", "item")),
            P(),
            P("item", None),
            P(),
            P("item", None),
            P(),
            P(None, "item"),
        ),
        out_specs=(P(("user", "item"), None), P(("user", "item"), None), P("item", "user")),
        check_vma=False,
    )
```

```python
import functools

import jax
import jax.numpy as jnp
from jax import lax
from jax.experimental import pallas as pl
from jax.experimental.pallas import tpu as pltpu
from jax.sharding import PartitionSpec as P

HEAD = 128
TOK_DEV = 256


norm_epsilon = 1e-05
scale_epsilon = 1e-06
inverse_temp = 20.0
loss_scale = 32.0


def layer_norm(values, gain):
    center = jnp.mean(values, axis=-1, keepdims=True)
    shifted = values - center
    spread = jnp.mean(shifted * shifted, axis=-1, keepdims=True)
    return shifted * lax.rsqrt(spread + norm_epsilon) * gain


def hstu_block(rows, segment, in_gain, w_uvqk, out_gain, w_out):
    count = rows.shape[0]
    rows_f = rows.astype(jnp.float32)
    normed = layer_norm(rows_f, in_gain).astype(jnp.bfloat16)
    projected = jnp.dot(
        normed,
        lax.all_gather(w_uvqk, "item", axis=0, tiled=True),
        preferred_element_type=jnp.float32,
    )
    active = jax.nn.silu(projected).astype(jnp.bfloat16)
    width = active.shape[1] // 4
    heads = width // HEAD
    gate_u = active[:, :width]
    values_v = active[:, width : 2 * width].reshape(count, heads, HEAD)
    queries = active[:, 2 * width : 3 * width].reshape(count, heads, HEAD)
    key_rows = active[:, 3 * width :].reshape(count, heads, HEAD)
    scores = jnp.einsum(
        "qhd,khd->hqk", queries, key_rows, preferred_element_type=jnp.float32
    ) * HEAD ** (-0.5)
    order = jnp.arange(count, dtype=jnp.int32)
    allowed = (segment[:, None] == segment[None, :]) & (order[None, :] <= order[:, None])
    weights = jnp.where(allowed[None], jax.nn.silu(scores), 0.0).astype(jnp.bfloat16)
    mixed = jnp.einsum(
        "hqk,khd->qhd", weights, values_v, preferred_element_type=jnp.float32
    ).reshape(count, width)
    gated = (layer_norm(mixed, out_gain) * gate_u.astype(jnp.float32)).astype(jnp.bfloat16)
    delta = jnp.dot(
        gated, lax.all_gather(w_out, "item", axis=1, tiled=True), preferred_element_type=jnp.float32
    )
    return (rows_f + delta).astype(jnp.bfloat16)


def dispatch(rows, home_start, history_len, targets, offsets, slot_rows, user_count):
    peers = jnp.arange(user_count, dtype=jnp.int32)
    chosen = (targets[None, :] == peers[:, None]).astype(jnp.int32)
    first_row = jnp.sum(chosen * home_start[None, :], axis=1)
    sent_count = jnp.sum(chosen * history_len[None, :], axis=1)
    landing = jnp.sum(chosen * offsets[None, :], axis=1)
    within = jnp.arange(slot_rows, dtype=jnp.int32)
    picked = jnp.minimum(first_row[:, None] + within[None, :], rows.shape[0] - 1)
    filled = within[None, :] < sent_count[:, None]
    parcels = jnp.where(filled[:, :, None], rows[picked], jnp.zeros((), rows.dtype))
    labels = jnp.stack([landing, sent_count], axis=1)
    arrived, arrived_labels = (
        lax.all_to_all(parcels, "user", split_axis=0, concat_axis=0, tiled=True),
        lax.all_to_all(labels, "user", split_axis=0, concat_axis=0, tiled=True),
    )
    worker_rows = jnp.arange(TOK_DEV, dtype=jnp.int32)
    lower = arrived_labels[:, 0]
    upper = lower + arrived_labels[:, 1]
    inside = (
        (worker_rows[:, None] >= lower[None, :]) & (worker_rows[:, None] < upper[None, :])
    ).astype(jnp.int32)
    source = jnp.sum(inside * peers[None, :], axis=1)
    begin = jnp.sum(inside * lower[None, :], axis=1)
    flattened = arrived.reshape(-1, arrived.shape[-1])
    gathered = flattened[source * slot_rows + worker_rows - begin]
    return (gathered, source, arrived_labels)


def per_device(
    tokens,
    lengths,
    destination,
    worker_offset,
    positives,
    negatives,
    table,
    in_gain,
    w_uvqk,
    out_gain,
    w_out,
):
    user_count = lax.axis_size("user")
    item_count = lax.axis_size("item")
    item_here = lax.axis_index("item")
    user_here = lax.axis_index("user")
    home_rows = tokens.shape[0]
    model_width = tokens.shape[1]
    hist_count = lengths.shape[1]
    slot_rows = home_rows // hist_count
    history_len = lengths[0]
    targets = destination[0]
    offsets = worker_offset[0]
    home_start = jnp.cumsum(history_len) - history_len
    row_ids = jnp.arange(home_rows, dtype=jnp.int32)
    finished = (row_ids[:, None] >= (home_start + history_len)[None, :]).astype(jnp.int32)
    home_segment = jnp.sum(finished, axis=1)
    valid = row_ids < jnp.sum(history_len)
    home_out = hstu_block(tokens, home_segment, in_gain, w_uvqk, out_gain, w_out)
    layer_out = dispatch(
        home_out, home_start, history_len, targets, offsets, slot_rows, user_count
    )[0]
    item_rows = table.shape[0]
    table_f = table.astype(jnp.float32)
    table_scale = lax.rsqrt(jnp.mean(table_f * table_f, axis=1) + scale_epsilon)
    table_hat = table_f * table_scale[:, None]
    table_low = table_hat.astype(jnp.bfloat16)
    share = negatives.shape[1] // item_count
    owned_ids = (
        lax.dynamic_slice_in_dim(negatives, item_here * share, share, 1) - item_here * item_rows
    )
    group_rows = lax.all_to_all(
        table_low[owned_ids], "item", split_axis=0, concat_axis=0, tiled=True
    ).reshape(-1, model_width)
    positive_local = positives - item_here * item_rows
    positive_rows = table_low[positive_local]
    out_f = home_out.astype(jnp.float32)
    out_scale = lax.rsqrt(jnp.mean(out_f * out_f, axis=1) + scale_epsilon)
    out_hat = out_f * out_scale[:, None]
    out_low = out_hat.astype(jnp.bfloat16)
    factor = inverse_temp / model_width
    positive_logit = (
        jnp.einsum("rd,rd->r", out_low, positive_rows, preferred_element_type=jnp.float32) * factor
    )
    negative_logit = (
        jnp.einsum("rd,nd->rn", out_low, group_rows, preferred_element_type=jnp.float32) * factor
    )
    positive_exp = jnp.exp(positive_logit)
    negative_exp = jnp.exp(negative_logit)
    partition = positive_exp + jnp.sum(negative_exp, axis=1)
    weight = jnp.where(valid, loss_scale, 0.0)
    positive_grad = weight * (positive_exp / partition - 1.0)
    negative_grad = (weight[:, None] * negative_exp / partition[:, None]).astype(jnp.bfloat16)
    grad_hat = (
        positive_grad[:, None] * positive_rows.astype(jnp.float32)
        + jnp.dot(negative_grad, group_rows, preferred_element_type=jnp.float32)
    ) * factor
    token_grad = (
        (grad_hat - out_hat * jnp.mean(grad_hat * out_hat, axis=1, keepdims=True))
        * out_scale[:, None]
    ).astype(jnp.bfloat16)
    negative_terms = (
        jnp.einsum("rn,rd->nd", negative_grad, out_low, preferred_element_type=jnp.float32) * factor
    )
    owned_terms = lax.all_to_all(
        negative_terms.reshape(item_count, share, model_width).astype(jnp.bfloat16),
        "item",
        split_axis=0,
        concat_axis=0,
        tiled=True,
    ).astype(jnp.float32)
    positive_terms = (positive_grad * factor)[:, None] * out_low.astype(jnp.float32)
    catalog = jnp.arange(item_rows, dtype=jnp.int32)
    positive_hits = (positive_local[None, :] == catalog[:, None]).astype(jnp.float32)
    negative_hits = (owned_ids.reshape(-1)[None, :] == catalog[:, None]).astype(jnp.float32)
    row_sums = jnp.dot(positive_hits, positive_terms, precision=lax.Precision.HIGHEST)
    row_sums = row_sums + jnp.dot(
        negative_hits, owned_terms.reshape(-1, model_width), precision=lax.Precision.HIGHEST
    )
    column_width = model_width // user_count
    totals = lax.psum(row_sums.astype(jnp.bfloat16), "user").astype(jnp.float32)
    inner = jnp.mean(totals * table_hat, axis=1)
    whole = (totals - table_hat * inner[:, None]) * table_scale[:, None]
    item_grad = lax.dynamic_slice_in_dim(whole, user_here * column_width, column_width, 1)
    return (layer_out, token_grad, item_grad)


MESH = pl.DeviceIdType.MESH
VMEM_SPEC = pl.BlockSpec(memory_space=pltpu.VMEM)


def remote(src, dst, send_sem, recv_sem, user, item):
    return pltpu.make_async_remote_copy(
        src_ref=src,
        dst_ref=dst,
        send_sem=send_sem,
        recv_sem=recv_sem,
        device_id=(user, item),
        device_id_type=MESH,
    )


def greet(users, items, u, i):
    barrier = pltpu.get_barrier_semaphore()
    for d in range(1, users):
        pl.semaphore_signal(
            barrier, inc=1, device_id=(lax.rem(u + d, users), i), device_id_type=MESH
        )
    for d in range(1, items):
        pl.semaphore_signal(
            barrier, inc=1, device_id=(u, lax.rem(i + d, items)), device_id_type=MESH
        )
    return barrier


def col_iota(shape):
    return lax.broadcasted_iota(jnp.int32, shape, 1)


def row_iota(shape):
    return lax.broadcasted_iota(jnp.int32, shape, 0)


def dot_f32(x, y, contract):
    return lax.dot_general(x, y, (contract, ((), ())), preferred_element_type=jnp.float32)


ROWS_T = ((0,), (0,))
PLAIN = ((1,), (0,))
COLS_T = ((1,), (1,))
TILE = 128


def fused_kernel(
    users, items,
    lens, dests, offs, tokens, pos, owned_ids, table, in_gain, w_ref, out_gain, o_ref,
    layer_out, token_grad, item_grad,
    wf, of, nf, lf, rows_out, labels, hat, low, scale, normed, allowed, pos_rows, pick_t,
    acc, active, mixed, home, parcels, arrived, out_low, hi, lo, ngrad, terms, owned, sums,
    chunks, got, inner_out, inner_got,
    own_sem, s1, r1, s2, r2, s3, r3, sn, rn, sl, rl, sd, rd, st, rt, sc, rc, si, ri,
):
    f32, bf16 = jnp.float32, jnp.bfloat16
    u = lax.axis_index("user")
    i = lax.axis_index("item")
    sibling = u + 1 - 2 * lax.rem(u, 2)
    half = users // 2
    count, width = tokens.shape
    hist = lens.shape[1]
    slot = count // hist
    cat = table.shape[0]
    share = owned_ids.shape[1] // items
    depth = width // items
    shard_cols = o_ref.shape[2]
    hd = active.shape[1] // 4
    cols = width // users
    factor = inverse_temp / width
    barrier = greet(users, items, u, i)

    ends = []
    total_len = jnp.int32(0)
    starts = []
    for h in range(hist):
        starts.append(total_len)
        total_len = total_len + lens[0, h]
        ends.append(total_len)

    def of_user(v, values):
        out = jnp.int32(0)
        for h in range(hist):
            out = out + jnp.where(dests[0, h] == v, values[h], 0)
        return out

    for v in range(users):
        landing = of_user(v, [offs[0, h] for h in range(hist)])
        sent_len = of_user(v, [lens[0, h] for h in range(hist)])
        labels[v] = jnp.where(row_iota((16, 128)) < 8, landing, sent_len)
    t_f = table[...].astype(f32)
    t_s = lax.rsqrt(jnp.mean(t_f * t_f, axis=1, keepdims=True) + scale_epsilon)
    scale[...] = t_s
    hat[...] = t_f * t_s
    low[...] = hat[...].astype(bf16)
    base = i * cat
    neg_hits = (row_iota((cat, items * share)) == owned_ids[...] - base).astype(bf16)
    rows_out[...] = dot_f32(neg_hits, low[...], ROWS_T).astype(bf16).reshape(rows_out.shape)

    pl.semaphore_wait(barrier, users + items - 2)
    pairs = ((w_ref, wf), (o_ref, of))
    sent = []

    def start(c):
        c.start()
        sent.append(c)

    for a, (src, dst) in enumerate(pairs):
        for d in range(1, items):
            start(remote(src.at[u], dst.at[i, u], s1.at[a, d - 1], r1.at[a, d - 1], u, lax.rem(i + d, items)))
    for d in range(1, items):
        i2 = lax.rem(i + d, items)
        start(remote(rows_out.at[i2], nf.at[i], sn.at[d - 1], rn.at[d - 1], u, i2))
    for d in range(1, users):
        u2 = lax.rem(u + d, users)
        start(remote(labels.at[u2], lf.at[u], sl.at[d - 1], rl.at[d - 1], u2, i))
    local = [
        pltpu.make_async_copy(o_ref, of.at[i], own_sem.at[0]),
        pltpu.make_async_copy(rows_out.at[i], nf.at[i], own_sem.at[1]),
        pltpu.make_async_copy(labels.at[u], lf.at[u], own_sem.at[2]),
    ]
    for c in local:
        c.start()

    def first_hop(a, d):
        dst = pairs[a][1]
        i2 = lax.rem(i + items - d, items)
        piece = dst.at[i2, u]
        remote(piece, piece, s1.at[a, d - 1], r1.at[a, d - 1], u, i2).wait_recv()
        for e in range(1, half):
            start(remote(piece, piece, s2.at[a, d - 1, e - 1], r2.at[a, d - 1, e - 1], lax.rem(u + 2 * e, users), i))
        start(remote(piece, piece, s3.at[a, d - 1, 0], r3.at[a, d - 1, 0], sibling, i))

    def second_hop(a, d):
        dst = pairs[a][1]
        i2 = lax.rem(i + items - d, items)
        for e in range(1, half):
            u2 = lax.rem(u + users - 2 * e, users)
            piece = dst.at[i2, u2]
            remote(piece, piece, s2.at[a, d - 1, e - 1], r2.at[a, d - 1, e - 1], u2, i).wait_recv()
            start(remote(piece, piece, s3.at[a, d - 1, e], r3.at[a, d - 1, e], sibling, i))

    def last_hop(a, d):
        dst = pairs[a][1]
        i2 = lax.rem(i + items - d, items)
        for e in range(half):
            piece = dst.at[i2, lax.rem(sibling + users - 2 * e, users)]
            remote(piece, piece, s3.at[a, d - 1, e], r3.at[a, d - 1, e], sibling, i).wait_recv()

    @pl.loop(0, count // TILE)
    def _(t):
        rs = pl.ds(pl.multiple_of(t * TILE, TILE), TILE)
        normed[rs, :] = layer_norm(tokens[rs, :].astype(f32), in_gain[...]).astype(bf16)

    wide = 256

    def project(d):
        i2 = lax.rem(i + items - d, items)
        x_cols = pl.ds(pl.multiple_of(i2 * depth, depth), depth)

        @pl.loop(0, active.shape[1] // wide)
        def _(t):
            cs = pl.ds(pl.multiple_of(t * wide, wide), wide)
            if d == 0:
                block = w_ref[:, :, cs].reshape(depth, wide)
            else:
                block = wf[i2, :, :, cs].reshape(depth, wide)
            part = dot_f32(normed[:, x_cols], block, PLAIN)
            if d == 0:
                acc[:, cs] = part
            elif d < items - 1:
                acc[:, cs] = acc[:, cs] + part
            else:
                active[:, cs] = jax.nn.silu(acc[:, cs] + part).astype(bf16)

    def prepare_mask():
        @pl.loop(0, count // TILE)
        def _(t):
            rows = row_iota((TILE, 2 * TILE)) + t * TILE
            keys = col_iota((TILE, 2 * TILE)) + (t - 1) * TILE
            row_seg = jnp.zeros_like(rows)
            key_seg = jnp.zeros_like(rows)
            for h in range(hist):
                row_seg = row_seg + (rows >= ends[h]).astype(jnp.int32)
                key_seg = key_seg + (keys >= ends[h]).astype(jnp.int32)
            ok = (row_seg == key_seg) & (keys <= rows) & (keys >= 0)
            allowed[t] = ok.astype(f32)

    def prepare_positives():
        pick_t[...] = (row_iota((cat, count)) == pos[...] - base).astype(bf16)

        @pl.loop(0, count // TILE)
        def _(t):
            rs = pl.ds(pl.multiple_of(t * TILE, TILE), TILE)
            pos_rows[rs, :] = dot_f32(pick_t[:, rs], low[...], ROWS_T).astype(bf16)

    extra = [prepare_positives, prepare_mask]
    project(0)
    for d in range(1, items):
        first_hop(0, d)
        if extra:
            extra.pop(0)()
    for work in extra:
        work()
    second_hop(0, 1)
    for d in range(1, items):
        first_hop(1, d)
    for d in range(1, items):
        if d + 1 < items:
            second_hop(0, d + 1)
        last_hop(0, d)
        project(d)
    for d in range(1, items):
        second_hop(1, d)

    @pl.loop(0, hd // HEAD)
    def _(h):
        def part_of(k):
            return pl.ds(pl.multiple_of(k * hd + h * HEAD, HEAD), HEAD)

        for t in range(count // TILE):
            first = max(t - 1, 0) * TILE
            keys = slice(first, (t + 1) * TILE)
            rows = slice(t * TILE, (t + 1) * TILE)
            s = dot_f32(active[rows, part_of(2)], active[keys, part_of(3)], COLS_T) * HEAD ** (-0.5)
            mask = allowed[t][:, 2 * TILE - s.shape[1] :]
            wgt = jnp.where(mask > 0.5, jax.nn.silu(s), 0.0).astype(bf16)
            mixed[rows, pl.ds(pl.multiple_of(h * HEAD, HEAD), HEAD)] = dot_f32(
                wgt, active[keys, part_of(1)], PLAIN
            )

    for c in local:
        c.wait()
    for d in range(1, items):
        last_hop(1, d)

    @pl.loop(0, count // TILE)
    def _(t):
        rs = pl.ds(pl.multiple_of(t * TILE, TILE), TILE)
        gated = (layer_norm(mixed[rs, :], out_gain[...]) * active[rs, :hd].astype(f32)).astype(bf16)
        for k in range(items):
            cs = slice(k * shard_cols, (k + 1) * shard_cols)
            delta = dot_f32(gated, of[k].reshape(hd, shard_cols), PLAIN)
            home[rs, cs] = (tokens[rs, cs].astype(f32) + delta).astype(bf16)

    @pl.loop(0, users)
    def _(v):
        begin = of_user(v, starts)
        sent_len = of_user(v, [lens[0, h] for h in range(hist)])
        k = row_iota((slot, count))
        pick = ((k + begin == col_iota((slot, count))) & (k < sent_len)).astype(bf16)
        parcels[v] = dot_f32(pick, home[...], PLAIN).astype(bf16)

    for d in range(1, users):
        u2 = lax.rem(u + d, users)
        start(remote(parcels.at[u2], arrived.at[u], sd.at[d - 1], rd.at[d - 1], u2, i))
    mine = pltpu.make_async_copy(parcels.at[u], arrived.at[u], own_sem.at[3])
    mine.start()
    for d in range(1, items):
        i2 = lax.rem(i + items - d, items)
        remote(nf.at[i2], nf.at[i2], sn.at[d - 1], rn.at[d - 1], u, i2).wait_recv()

    @pl.loop(0, count // TILE)
    def _(t):
        rs = pl.ds(pl.multiple_of(t * TILE, TILE), TILE)
        group = nf[...].reshape(items * share, width)
        out_f = home[rs, :].astype(f32)
        out_scale = lax.rsqrt(jnp.mean(out_f * out_f, axis=1, keepdims=True) + scale_epsilon)
        out_hat = out_f * out_scale
        o_low = out_hat.astype(bf16)
        out_low[rs, :] = o_low
        o_low_f = o_low.astype(f32)
        p_rows = pos_rows[rs, :].astype(f32)
        pos_logit = jnp.sum(o_low_f * p_rows, axis=1, keepdims=True) * factor
        neg_logit = dot_f32(o_low, group, COLS_T) * factor
        pos_exp = jnp.exp(pos_logit)
        neg_exp = jnp.exp(neg_logit)
        partition = pos_exp + jnp.sum(neg_exp, axis=1, keepdims=True)
        ids = row_iota((TILE, 1)) + t * TILE
        weight = jnp.where(ids < total_len, loss_scale, 0.0)
        pos_grad = weight * (pos_exp / partition - 1.0)
        n_grad = (weight * neg_exp / partition).astype(bf16)
        ngrad[rs, :] = n_grad
        grad_hat = (pos_grad * p_rows + dot_f32(n_grad, group, PLAIN)) * factor
        inner = jnp.mean(grad_hat * out_hat, axis=1, keepdims=True)
        token_grad[rs, :] = ((grad_hat - out_hat * inner) * out_scale).astype(bf16)
        pos_terms = (pos_grad * factor) * o_low_f
        top = pos_terms.astype(bf16)
        hi[rs, :] = top
        lo[rs, :] = (pos_terms - top.astype(f32)).astype(bf16)

    terms[...] = (dot_f32(ngrad[...], out_low[...], ROWS_T) * factor).astype(bf16).reshape(terms.shape)
    sums[...] = dot_f32(pick_t[...], hi[...], PLAIN)
    for d in range(1, items):
        i2 = lax.rem(i + d, items)
        start(remote(terms.at[i2], owned.at[i], st.at[d - 1], rt.at[d - 1], u, i2))
    own = pltpu.make_async_copy(terms.at[i], owned.at[i], own_sem.at[4])
    own.start()
    sums[...] = sums[...] + dot_f32(pick_t[...], lo[...], PLAIN)
    hits = (row_iota((cat, items * share)) == owned_ids[...] - base).astype(bf16)
    own.wait()
    for d in range(1, items):
        i2 = lax.rem(i + items - d, items)
        remote(owned.at[i2], owned.at[i2], st.at[d - 1], rt.at[d - 1], u, i2).wait_recv()
    row_sums = sums[...] + dot_f32(hits, owned[...].reshape(items * share, width), PLAIN)
    for v in range(users):
        chunks[v] = row_sums[:, v * cols : (v + 1) * cols].astype(bf16)
    inner = jnp.mean(row_sums * hat[...], axis=1, keepdims=True)
    inner_out[...] = jnp.transpose(jnp.broadcast_to(inner, (cat, 128)))[:8]
    for d in range(1, users):
        u2 = lax.rem(u + d, users)
        start(remote(chunks.at[u2], got.at[u], sc.at[d - 1], rc.at[d - 1], u2, i))
        start(remote(inner_out, inner_got.at[u], si.at[d - 1], ri.at[d - 1], u2, i))
    mine.wait()
    for d in range(1, users):
        u2 = lax.rem(u + users - d, users)
        remote(lf.at[u2], lf.at[u2], sl.at[d - 1], rl.at[d - 1], u2, i).wait_recv()
        remote(arrived.at[u2], arrived.at[u2], sd.at[d - 1], rd.at[d - 1], u2, i).wait_recv()
    worker_rows = layer_out.shape[0]
    laid = jnp.zeros((worker_rows, width), f32)
    for v in range(0, users, 2):
        k = col_iota((worker_rows, 2 * slot))
        second = k >= slot
        k = k - jnp.where(second, slot, 0)
        begin = jnp.where(second, lf[v + 1][:1, : 2 * slot], lf[v][:1, : 2 * slot])
        sent_len = jnp.where(second, lf[v + 1][8:9, : 2 * slot], lf[v][8:9, : 2 * slot])
        place = ((k + begin == row_iota((worker_rows, 2 * slot))) & (k < sent_len)).astype(bf16)
        laid = laid + dot_f32(place, arrived[v : v + 2].reshape(2 * slot, width), PLAIN)
    layer_out[...] = laid.astype(bf16)
    total = chunks[u].astype(f32)
    inner_total = inner_out[...]
    for d in range(1, users):
        u2 = lax.rem(u + users - d, users)
        remote(got.at[u2], got.at[u2], sc.at[d - 1], rc.at[d - 1], u2, i).wait_recv()
        remote(inner_got.at[u2], inner_got.at[u2], si.at[d - 1], ri.at[d - 1], u2, i).wait_recv()
        total = total + got[u2].astype(f32)
        inner_total = inner_total + inner_got[u2]
    inner_rows = jnp.transpose(jnp.broadcast_to(inner_total[:1], (128, cat)))
    here = hat[:, pl.ds(pl.multiple_of(u * cols, cols), cols)]
    item_grad[...] = (total - here * inner_rows[:, :cols]) * scale[...]
    for c in sent:
        c.wait_send()


def fused(
    users, items,
    tokens, lengths, destination, worker_offset, positives, negatives, table,
    in_gain, w_uvqk, out_gain, w_out,
):
    f32, bf16 = jnp.float32, jnp.bfloat16
    dma = pltpu.SemaphoreType.DMA
    half = users // 2
    count, width = tokens.shape
    slot = count // lengths.shape[1]
    share = negatives.shape[1] // items
    cat = table.shape[0]
    cols = width // users
    total = w_uvqk.shape[1]
    hd = out_gain.shape[0]
    ids = lax.dynamic_slice_in_dim(
        negatives, lax.axis_index("item") * share, share, 1
    ).reshape(1, -1)
    w3 = w_uvqk.reshape(users, w_uvqk.shape[0] // users, total)
    o3 = w_out.reshape(users, w_out.shape[0] // users, w_out.shape[1])
    smem = pl.BlockSpec(memory_space=pltpu.SMEM)
    return pl.pallas_call(
        functools.partial(fused_kernel, users, items),
        out_shape=(
            jax.ShapeDtypeStruct((TOK_DEV, width), bf16),
            jax.ShapeDtypeStruct((count, width), bf16),
            jax.ShapeDtypeStruct((cat, cols), f32),
        ),
        in_specs=[smem] * 3 + [VMEM_SPEC] * 8,
        out_specs=(VMEM_SPEC,) * 3,
        scratch_shapes=[
            pltpu.VMEM((items,) + w3.shape, bf16),
            pltpu.VMEM((items,) + o3.shape, bf16),
            pltpu.VMEM((items, share, width), bf16),
            pltpu.VMEM((users, 16, 128), jnp.int32),
            pltpu.VMEM((items, share, width), bf16),
            pltpu.VMEM((users, 16, 128), jnp.int32),
            pltpu.VMEM((cat, width), f32),
            pltpu.VMEM((cat, width), bf16),
            pltpu.VMEM((cat, 1), f32),
            pltpu.VMEM((count, width), bf16),
            pltpu.VMEM((count // TILE, TILE, 2 * TILE), f32),
            pltpu.VMEM((count, width), bf16),
            pltpu.VMEM((cat, count), bf16),
            pltpu.VMEM((count, total), f32),
            pltpu.VMEM((count, total), bf16),
            pltpu.VMEM((count, hd), f32),
            pltpu.VMEM((count, width), bf16),
            pltpu.VMEM((users, slot, width), bf16),
            pltpu.VMEM((users, slot, width), bf16),
            pltpu.VMEM((count, width), bf16),
            pltpu.VMEM((count, width), bf16),
            pltpu.VMEM((count, width), bf16),
            pltpu.VMEM((count, items * share), bf16),
            pltpu.VMEM((items, share, width), bf16),
            pltpu.VMEM((items, share, width), bf16),
            pltpu.VMEM((cat, width), f32),
            pltpu.VMEM((users, cat, cols), bf16),
            pltpu.VMEM((users, cat, cols), bf16),
            pltpu.VMEM((8, cat), f32),
            pltpu.VMEM((users, 8, cat), f32),
            dma((5,)),
            dma((2, items - 1)), dma((2, items - 1)),
            dma((2, items - 1, half - 1)), dma((2, items - 1, half - 1)),
            dma((2, items - 1, half)), dma((2, items - 1, half)),
            dma((items - 1,)), dma((items - 1,)),
            dma((users - 1,)), dma((users - 1,)),
            dma((users - 1,)), dma((users - 1,)),
            dma((items - 1,)), dma((items - 1,)),
            dma((users - 1,)), dma((users - 1,)),
            dma((users - 1,)), dma((users - 1,)),
        ],
        compiler_params=pltpu.CompilerParams(
            collective_id=0, has_side_effects=True, vmem_limit_bytes=60 << 20
        ),
    )(
        lengths, destination, worker_offset, tokens, positives.reshape(1, -1), ids, table,
        in_gain.reshape(1, -1), w3, out_gain.reshape(1, -1), o3,
    )


def step(users, items, tokens, lengths, destination, worker_offset, positives, negatives, table,
         in_gain, w_uvqk, out_gain, w_out):
    aligned = (
        users % 2 == 0
        and users > 2
        and tokens.shape[0] % TILE == 0
        and tokens.shape[0] // lengths.shape[1] <= TILE // 2
        and table.shape[0] % 256 == 0
        and items > 1
        and w_uvqk.shape[0] % (16 * users) == 0
        and w_out.shape[0] % (16 * users) == 0
        and w_out.shape[1] % 128 == 0
        and tokens.shape[1] == 128 * users
        and table.shape[0] % 128 == 0
        and negatives.shape[1] % (16 * items) == 0
    )
    run = functools.partial(fused, users, items) if aligned else per_device
    return run(tokens, lengths, destination, worker_offset, positives, negatives, table,
               in_gain, w_uvqk, out_gain, w_out)


def solution(mesh):
    return jax.shard_map(
        functools.partial(step, mesh.shape["user"], mesh.shape["item"]),
        mesh=mesh,
        in_specs=(
            P(("user", "item"), None),
            P(("user", "item"), None),
            P(("user", "item"), None),
            P(("user", "item"), None),
            P(("user", "item")),
            P(),
            P("item", None),
            P(),
            P("item", None),
            P(),
            P(None, "item"),
        ),
        out_specs=(P(("user", "item"), None), P(("user", "item"), None), P("item", "user")),
        check_vma=False,
    )
```

```python
import functools

import jax
import jax.numpy as jnp
from jax import lax
from jax.experimental import pallas as pl
from jax.experimental.pallas import tpu as pltpu
from jax.sharding import PartitionSpec as P

HEAD = 128
TOK_DEV = 256


norm_epsilon = 1e-05
scale_epsilon = 1e-06
inverse_temp = 20.0
loss_scale = 32.0


def layer_norm(values, gain):
    center = jnp.mean(values, axis=-1, keepdims=True)
    shifted = values - center
    spread = jnp.mean(shifted * shifted, axis=-1, keepdims=True)
    return shifted * lax.rsqrt(spread + norm_epsilon) * gain


def hstu_block(rows, segment, in_gain, w_uvqk, out_gain, w_out):
    count = rows.shape[0]
    rows_f = rows.astype(jnp.float32)
    normed = layer_norm(rows_f, in_gain).astype(jnp.bfloat16)
    projected = jnp.dot(
        normed,
        lax.all_gather(w_uvqk, "item", axis=0, tiled=True),
        preferred_element_type=jnp.float32,
    )
    active = jax.nn.silu(projected).astype(jnp.bfloat16)
    width = active.shape[1] // 4
    heads = width // HEAD
    gate_u = active[:, :width]
    values_v = active[:, width : 2 * width].reshape(count, heads, HEAD)
    queries = active[:, 2 * width : 3 * width].reshape(count, heads, HEAD)
    key_rows = active[:, 3 * width :].reshape(count, heads, HEAD)
    scores = jnp.einsum(
        "qhd,khd->hqk", queries, key_rows, preferred_element_type=jnp.float32
    ) * HEAD ** (-0.5)
    order = jnp.arange(count, dtype=jnp.int32)
    allowed = (segment[:, None] == segment[None, :]) & (order[None, :] <= order[:, None])
    weights = jnp.where(allowed[None], jax.nn.silu(scores), 0.0).astype(jnp.bfloat16)
    mixed = jnp.einsum(
        "hqk,khd->qhd", weights, values_v, preferred_element_type=jnp.float32
    ).reshape(count, width)
    gated = (layer_norm(mixed, out_gain) * gate_u.astype(jnp.float32)).astype(jnp.bfloat16)
    delta = jnp.dot(
        gated, lax.all_gather(w_out, "item", axis=1, tiled=True), preferred_element_type=jnp.float32
    )
    return (rows_f + delta).astype(jnp.bfloat16)


def dispatch(rows, home_start, history_len, targets, offsets, slot_rows, user_count):
    peers = jnp.arange(user_count, dtype=jnp.int32)
    chosen = (targets[None, :] == peers[:, None]).astype(jnp.int32)
    first_row = jnp.sum(chosen * home_start[None, :], axis=1)
    sent_count = jnp.sum(chosen * history_len[None, :], axis=1)
    landing = jnp.sum(chosen * offsets[None, :], axis=1)
    within = jnp.arange(slot_rows, dtype=jnp.int32)
    picked = jnp.minimum(first_row[:, None] + within[None, :], rows.shape[0] - 1)
    filled = within[None, :] < sent_count[:, None]
    parcels = jnp.where(filled[:, :, None], rows[picked], jnp.zeros((), rows.dtype))
    labels = jnp.stack([landing, sent_count], axis=1)
    arrived, arrived_labels = (
        lax.all_to_all(parcels, "user", split_axis=0, concat_axis=0, tiled=True),
        lax.all_to_all(labels, "user", split_axis=0, concat_axis=0, tiled=True),
    )
    worker_rows = jnp.arange(TOK_DEV, dtype=jnp.int32)
    lower = arrived_labels[:, 0]
    upper = lower + arrived_labels[:, 1]
    inside = (
        (worker_rows[:, None] >= lower[None, :]) & (worker_rows[:, None] < upper[None, :])
    ).astype(jnp.int32)
    source = jnp.sum(inside * peers[None, :], axis=1)
    begin = jnp.sum(inside * lower[None, :], axis=1)
    flattened = arrived.reshape(-1, arrived.shape[-1])
    gathered = flattened[source * slot_rows + worker_rows - begin]
    return (gathered, source, arrived_labels)


def per_device(
    tokens,
    lengths,
    destination,
    worker_offset,
    positives,
    negatives,
    table,
    in_gain,
    w_uvqk,
    out_gain,
    w_out,
):
    user_count = lax.axis_size("user")
    item_count = lax.axis_size("item")
    item_here = lax.axis_index("item")
    user_here = lax.axis_index("user")
    home_rows = tokens.shape[0]
    model_width = tokens.shape[1]
    hist_count = lengths.shape[1]
    slot_rows = home_rows // hist_count
    history_len = lengths[0]
    targets = destination[0]
    offsets = worker_offset[0]
    home_start = jnp.cumsum(history_len) - history_len
    row_ids = jnp.arange(home_rows, dtype=jnp.int32)
    finished = (row_ids[:, None] >= (home_start + history_len)[None, :]).astype(jnp.int32)
    home_segment = jnp.sum(finished, axis=1)
    valid = row_ids < jnp.sum(history_len)
    home_out = hstu_block(tokens, home_segment, in_gain, w_uvqk, out_gain, w_out)
    layer_out = dispatch(
        home_out, home_start, history_len, targets, offsets, slot_rows, user_count
    )[0]
    item_rows = table.shape[0]
    table_f = table.astype(jnp.float32)
    table_scale = lax.rsqrt(jnp.mean(table_f * table_f, axis=1) + scale_epsilon)
    table_hat = table_f * table_scale[:, None]
    table_low = table_hat.astype(jnp.bfloat16)
    share = negatives.shape[1] // item_count
    owned_ids = (
        lax.dynamic_slice_in_dim(negatives, item_here * share, share, 1) - item_here * item_rows
    )
    group_rows = lax.all_to_all(
        table_low[owned_ids], "item", split_axis=0, concat_axis=0, tiled=True
    ).reshape(-1, model_width)
    positive_local = positives - item_here * item_rows
    positive_rows = table_low[positive_local]
    out_f = home_out.astype(jnp.float32)
    out_scale = lax.rsqrt(jnp.mean(out_f * out_f, axis=1) + scale_epsilon)
    out_hat = out_f * out_scale[:, None]
    out_low = out_hat.astype(jnp.bfloat16)
    factor = inverse_temp / model_width
    positive_logit = (
        jnp.einsum("rd,rd->r", out_low, positive_rows, preferred_element_type=jnp.float32) * factor
    )
    negative_logit = (
        jnp.einsum("rd,nd->rn", out_low, group_rows, preferred_element_type=jnp.float32) * factor
    )
    positive_exp = jnp.exp(positive_logit)
    negative_exp = jnp.exp(negative_logit)
    partition = positive_exp + jnp.sum(negative_exp, axis=1)
    weight = jnp.where(valid, loss_scale, 0.0)
    positive_grad = weight * (positive_exp / partition - 1.0)
    negative_grad = (weight[:, None] * negative_exp / partition[:, None]).astype(jnp.bfloat16)
    grad_hat = (
        positive_grad[:, None] * positive_rows.astype(jnp.float32)
        + jnp.dot(negative_grad, group_rows, preferred_element_type=jnp.float32)
    ) * factor
    token_grad = (
        (grad_hat - out_hat * jnp.mean(grad_hat * out_hat, axis=1, keepdims=True))
        * out_scale[:, None]
    ).astype(jnp.bfloat16)
    negative_terms = (
        jnp.einsum("rn,rd->nd", negative_grad, out_low, preferred_element_type=jnp.float32) * factor
    )
    owned_terms = lax.all_to_all(
        negative_terms.reshape(item_count, share, model_width).astype(jnp.bfloat16),
        "item",
        split_axis=0,
        concat_axis=0,
        tiled=True,
    ).astype(jnp.float32)
    positive_terms = (positive_grad * factor)[:, None] * out_low.astype(jnp.float32)
    catalog = jnp.arange(item_rows, dtype=jnp.int32)
    positive_hits = (positive_local[None, :] == catalog[:, None]).astype(jnp.float32)
    negative_hits = (owned_ids.reshape(-1)[None, :] == catalog[:, None]).astype(jnp.float32)
    row_sums = jnp.dot(positive_hits, positive_terms, precision=lax.Precision.HIGHEST)
    row_sums = row_sums + jnp.dot(
        negative_hits, owned_terms.reshape(-1, model_width), precision=lax.Precision.HIGHEST
    )
    column_width = model_width // user_count
    totals = lax.psum(row_sums.astype(jnp.bfloat16), "user").astype(jnp.float32)
    inner = jnp.mean(totals * table_hat, axis=1)
    whole = (totals - table_hat * inner[:, None]) * table_scale[:, None]
    item_grad = lax.dynamic_slice_in_dim(whole, user_here * column_width, column_width, 1)
    return (layer_out, token_grad, item_grad)


MESH = pl.DeviceIdType.MESH
VMEM_SPEC = pl.BlockSpec(memory_space=pltpu.VMEM)


def remote(src, dst, send_sem, recv_sem, user, item):
    return pltpu.make_async_remote_copy(
        src_ref=src,
        dst_ref=dst,
        send_sem=send_sem,
        recv_sem=recv_sem,
        device_id=(user, item),
        device_id_type=MESH,
    )


def greet(users, items, u, i):
    barrier = pltpu.get_barrier_semaphore()
    for d in range(1, users):
        pl.semaphore_signal(
            barrier, inc=1, device_id=(lax.rem(u + d, users), i), device_id_type=MESH
        )
    for d in range(1, items):
        pl.semaphore_signal(
            barrier, inc=1, device_id=(u, lax.rem(i + d, items)), device_id_type=MESH
        )
    return barrier


def col_iota(shape):
    return lax.broadcasted_iota(jnp.int32, shape, 1)


def row_iota(shape):
    return lax.broadcasted_iota(jnp.int32, shape, 0)


def dot_f32(x, y, contract):
    return lax.dot_general(x, y, (contract, ((), ())), preferred_element_type=jnp.float32)


ROWS_T = ((0,), (0,))
PLAIN = ((1,), (0,))
COLS_T = ((1,), (1,))
TILE = 128


def fused_kernel(
    users, items,
    lens, dests, offs, tokens, pos, negs, table, in_gain, w_ref, out_gain, o_ref,
    layer_out, token_grad, item_grad,
    wf, of, nf, lf, rows_out, labels, hat, low, scale, normed, allowed, pos_rows, pick_t,
    acc, active, mixed, home, parcels, arrived, out_low, hi, lo, ngrad, terms, owned, sums,
    chunks, got, inner_out, inner_got, kept,
    own_sem, s1, r1, s2, r2, s3, r3, s4, r4, sn, rn, sl, rl, sd, rd, st, rt, sc, rc, si, ri,
):
    f32, bf16 = jnp.float32, jnp.bfloat16
    u = lax.axis_index("user")
    i = lax.axis_index("item")
    half = users // 2

    def flip(v, bit):
        return v + bit - 2 * bit * lax.rem(v // bit, 2)

    sibling, near_x, near_y = flip(u, 1), flip(u, 2), flip(u, 4)
    across = flip(near_x, 4)
    count, width = tokens.shape
    hist = lens.shape[1]
    slot = count // hist
    cat = table.shape[0]
    share = negs.shape[1] // items
    depth = width // items
    shard_cols = o_ref.shape[2]
    hd = active.shape[1] // 4
    cols = width // users
    factor = inverse_temp / width
    barrier = greet(users, items, u, i)

    ends = []
    total_len = jnp.int32(0)
    starts = []
    for h in range(hist):
        starts.append(total_len)
        total_len = total_len + lens[0, h]
        ends.append(total_len)

    def of_user(v, values):
        out = jnp.int32(0)
        for h in range(hist):
            out = out + jnp.where(dests[0, h] == v, values[h], 0)
        return out

    for v in range(users):
        landing = of_user(v, [offs[0, h] for h in range(hist)])
        sent_len = of_user(v, [lens[0, h] for h in range(hist)])
        labels[v] = jnp.where(row_iota((16, 128)) < 8, landing, sent_len)
    t_f = table[...].astype(f32)
    t_s = lax.rsqrt(jnp.mean(t_f * t_f, axis=1, keepdims=True) + scale_epsilon)
    scale[...] = t_s
    hat[...] = t_f * t_s
    low[...] = hat[...].astype(bf16)
    base = i * cat
    owned_ids = []
    for g in range(items):
        mine_ids = negs[g : g + 1, :share]
        for k in range(1, items):
            mine_ids = jnp.where(i == k, negs[g : g + 1, k * share : (k + 1) * share], mine_ids)
        owned_ids.append(mine_ids - base)
    owned_ids = jnp.concatenate(owned_ids, axis=1)
    neg_hits = (row_iota((cat, items * share)) == owned_ids).astype(bf16)
    rows_out[...] = dot_f32(neg_hits, low[...], ROWS_T).astype(bf16).reshape(rows_out.shape)

    pl.semaphore_wait(barrier, users + items - 2)
    pairs = ((w_ref, wf), (o_ref, of))
    sent = []

    def start(c):
        c.start()
        sent.append(c)

    for a, (src, dst) in enumerate(pairs):
        for d in range(1, items):
            start(remote(src.at[u], dst.at[i, u], s1.at[a, d - 1], r1.at[a, d - 1], u, lax.rem(i + d, items)))
    for d in range(1, items):
        i2 = lax.rem(i + d, items)
        start(remote(rows_out.at[i2], nf.at[i], sn.at[d - 1], rn.at[d - 1], u, i2))
    for d in range(1, users):
        u2 = lax.rem(u + d, users)
        start(remote(labels.at[u2], lf.at[u], sl.at[d - 1], rl.at[d - 1], u2, i))
    local = [
        pltpu.make_async_copy(o_ref, of.at[i], own_sem.at[0]),
        pltpu.make_async_copy(rows_out.at[i], nf.at[i], own_sem.at[1]),
        pltpu.make_async_copy(labels.at[u], lf.at[u], own_sem.at[2]),
        pltpu.make_async_copy(w_ref, wf.at[i], own_sem.at[5]),
    ]
    for c in local:
        c.start()

    def place_of(a, d, v):
        return pairs[a][1].at[lax.rem(i + items - d, items), v]

    def halves(a, d, v):
        rows = pairs[a][1].shape[2]
        i2 = lax.rem(i + items - d, items)
        return [pairs[a][1].at[i2, v, : rows // 2], pairs[a][1].at[i2, v, rows // 2 :]]

    def move(piece, ss, rr, a, d, e, v):
        return remote(piece, piece, ss.at[a, d - 1, e], rr.at[a, d - 1, e], v, i)

    def first_hop(a, d):
        piece = place_of(a, d, u)
        i2 = lax.rem(i + items - d, items)
        remote(piece, piece, s1.at[a, d - 1], r1.at[a, d - 1], u, i2).wait_recv()
        start(move(piece, s2, r2, a, d, 0, near_x))
        start(move(piece, s2, r2, a, d, 1, near_y))
        start(move(piece, s3, r3, a, d, 0, sibling))

    def second_hop(a, d):
        piece = place_of(a, d, near_x)
        move(piece, s2, r2, a, d, 0, near_x).wait_recv()
        start(move(halves(a, d, near_x)[0], s4, r4, a, d, 0, near_y))
        start(move(piece, s3, r3, a, d, 1, sibling))
        piece = place_of(a, d, near_y)
        move(piece, s2, r2, a, d, 1, near_y).wait_recv()
        start(move(halves(a, d, near_y)[1], s4, r4, a, d, 1, near_x))
        start(move(piece, s3, r3, a, d, 2, sibling))

    def third_hop(a, d):
        first, second = halves(a, d, across)
        move(first, s4, r4, a, d, 0, near_y).wait_recv()
        move(second, s4, r4, a, d, 1, near_x).wait_recv()
        start(move(place_of(a, d, across), s3, r3, a, d, 3, sibling))

    def last_hop(a, d):
        for e, v in enumerate((sibling, flip(sibling, 2), flip(sibling, 4), flip(flip(sibling, 2), 4))):
            move(place_of(a, d, v), s3, r3, a, d, e, sibling).wait_recv()

    @pl.loop(0, count // TILE)
    def _(t):
        rs = pl.ds(pl.multiple_of(t * TILE, TILE), TILE)
        normed[rs, :] = layer_norm(tokens[rs, :].astype(f32), in_gain[...]).astype(bf16)

    wide = 256

    def project(d):
        i2 = lax.rem(i + items - d, items)
        x_cols = pl.ds(pl.multiple_of(i2 * depth, depth), depth)

        @pl.loop(0, active.shape[1] // wide)
        def _(t):
            cs = pl.ds(pl.multiple_of(t * wide, wide), wide)
            block = wf[i2, :, :, cs].reshape(depth, wide)
            part = dot_f32(normed[:, x_cols], block, PLAIN)
            if d == 0:
                acc[:, cs] = part
            elif d < items - 1:
                acc[:, cs] = acc[:, cs] + part
            else:
                active[:, cs] = jax.nn.silu(acc[:, cs] + part).astype(bf16)

    def prepare_mask():
        @pl.loop(0, count // TILE)
        def _(t):
            rows = row_iota((TILE, 2 * TILE)) + t * TILE
            keys = col_iota((TILE, 2 * TILE)) + (t - 1) * TILE
            row_seg = jnp.zeros_like(rows)
            key_seg = jnp.zeros_like(rows)
            for h in range(hist):
                row_seg = row_seg + (rows >= ends[h]).astype(jnp.int32)
                key_seg = key_seg + (keys >= ends[h]).astype(jnp.int32)
            ok = (row_seg == key_seg) & (keys <= rows) & (keys >= 0)
            allowed[t] = ok.astype(f32)

    def prepare_positives():
        pick_t[...] = (row_iota((cat, count)) == pos[...] - base).astype(bf16)

        @pl.loop(0, count // TILE)
        def _(t):
            rs = pl.ds(pl.multiple_of(t * TILE, TILE), TILE)
            pos_rows[rs, :] = dot_f32(pick_t[:, rs], low[...], ROWS_T).astype(bf16)

    steps = range(1, items)
    local[3].wait()
    project(0)
    for d in steps:
        first_hop(0, d)
        if d == 1:
            prepare_positives()
            prepare_mask()
        else:
            second_hop(0, d - 1)
    first_hop(1, 1)
    third_hop(0, 1)
    second_hop(0, items - 1)
    for d in steps:
        if d > 1:
            first_hop(1, d)
            third_hop(0, d)
        if d == items - 1:
            for k in steps:
                second_hop(1, k)
        last_hop(0, d)
        project(d)
    for d in steps:
        third_hop(1, d)

    @pl.loop(0, hd // HEAD)
    def _(h):
        def part_of(k):
            return pl.ds(pl.multiple_of(k * hd + h * HEAD, HEAD), HEAD)

        for t in range(count // TILE):
            first = max(t - 1, 0) * TILE
            keys = slice(first, (t + 1) * TILE)
            rows = slice(t * TILE, (t + 1) * TILE)
            s = dot_f32(active[rows, part_of(2)], active[keys, part_of(3)], COLS_T) * HEAD ** (-0.5)
            mask = allowed[t][:, 2 * TILE - s.shape[1] :]
            wgt = jnp.where(mask > 0.5, jax.nn.silu(s), 0.0).astype(bf16)
            mixed[rows, pl.ds(pl.multiple_of(h * HEAD, HEAD), HEAD)] = dot_f32(
                wgt, active[keys, part_of(1)], PLAIN
            )

    for c in local[:3]:
        c.wait()
    for d in range(1, items):
        last_hop(1, d)

    @pl.loop(0, count // TILE)
    def _(t):
        rs = pl.ds(pl.multiple_of(t * TILE, TILE), TILE)
        gated = (layer_norm(mixed[rs, :], out_gain[...]) * active[rs, :hd].astype(f32)).astype(bf16)
        for k in range(items):
            cs = slice(k * shard_cols, (k + 1) * shard_cols)
            delta = dot_f32(gated, of[k].reshape(hd, shard_cols), PLAIN)
            home[rs, cs] = (tokens[rs, cs].astype(f32) + delta).astype(bf16)

    for d in range(1, items):
        i2 = lax.rem(i + items - d, items)
        remote(nf.at[i2], nf.at[i2], sn.at[d - 1], rn.at[d - 1], u, i2).wait_recv()

    @pl.loop(0, count // TILE)
    def _(t):
        rs = pl.ds(pl.multiple_of(t * TILE, TILE), TILE)
        group = nf[...].reshape(items * share, width)
        out_f = home[rs, :].astype(f32)
        out_scale = lax.rsqrt(jnp.mean(out_f * out_f, axis=1, keepdims=True) + scale_epsilon)
        o_low = (out_f * out_scale).astype(bf16)
        out_low[rs, :] = o_low
        pos_logit = (
            jnp.sum(o_low.astype(f32) * pos_rows[rs, :].astype(f32), axis=1, keepdims=True) * factor
        )
        neg_exp = jnp.exp(dot_f32(o_low, group, COLS_T) * factor)
        pos_exp = jnp.exp(pos_logit)
        partition = pos_exp + jnp.sum(neg_exp, axis=1, keepdims=True)
        ids = row_iota((TILE, 1)) + t * TILE
        weight = jnp.where(ids < total_len, loss_scale, 0.0)
        pos_grad = weight * (pos_exp / partition - 1.0)
        ngrad[rs, :] = (weight * neg_exp / partition).astype(bf16)
        kept[rs, :] = jnp.where(col_iota((TILE, 128)) == 0, pos_grad, out_scale)

    terms[...] = (dot_f32(ngrad[...], out_low[...], ROWS_T) * factor).astype(bf16).reshape(terms.shape)
    for d in range(1, items):
        i2 = lax.rem(i + d, items)
        start(remote(terms.at[i2], owned.at[i], st.at[d - 1], rt.at[d - 1], u, i2))
    own = pltpu.make_async_copy(terms.at[i], owned.at[i], own_sem.at[4])
    own.start()

    @pl.loop(0, users)
    def _(v):
        begin = of_user(v, starts)
        sent_len = of_user(v, [lens[0, h] for h in range(hist)])
        k = row_iota((slot, count))
        pick = ((k + begin == col_iota((slot, count))) & (k < sent_len)).astype(bf16)
        parcels[v] = dot_f32(pick, home[...], PLAIN).astype(bf16)

    for d in range(1, users):
        u2 = lax.rem(u + d, users)
        start(remote(parcels.at[u2], arrived.at[u], sd.at[d - 1], rd.at[d - 1], u2, i))
    mine = pltpu.make_async_copy(parcels.at[u], arrived.at[u], own_sem.at[3])
    mine.start()

    @pl.loop(0, count // TILE)
    def _(t):
        rs = pl.ds(pl.multiple_of(t * TILE, TILE), TILE)
        group = nf[...].reshape(items * share, width)
        pos_grad = kept[rs, :1]
        out_scale = kept[rs, 1:2]
        pos_terms = (pos_grad * factor) * out_low[rs, :].astype(f32)
        top = pos_terms.astype(bf16)
        hi[rs, :] = top
        lo[rs, :] = (pos_terms - top.astype(f32)).astype(bf16)
        out_hat = home[rs, :].astype(f32) * out_scale
        grad_hat = (
            pos_grad * pos_rows[rs, :].astype(f32) + dot_f32(ngrad[rs, :], group, PLAIN)
        ) * factor
        inner = jnp.mean(grad_hat * out_hat, axis=1, keepdims=True)
        token_grad[rs, :] = ((grad_hat - out_hat * inner) * out_scale).astype(bf16)

    sums[...] = dot_f32(pick_t[...], hi[...], PLAIN) + dot_f32(pick_t[...], lo[...], PLAIN)
    hits = (row_iota((cat, items * share)) == owned_ids).astype(bf16)
    own.wait()
    for d in range(1, items):
        i2 = lax.rem(i + items - d, items)
        remote(owned.at[i2], owned.at[i2], st.at[d - 1], rt.at[d - 1], u, i2).wait_recv()
    row_sums = sums[...] + dot_f32(hits, owned[...].reshape(items * share, width), PLAIN)
    for v in range(users):
        chunks[v] = row_sums[:, v * cols : (v + 1) * cols].astype(bf16)
    inner = jnp.mean(row_sums * hat[...], axis=1, keepdims=True)
    inner_out[...] = jnp.transpose(jnp.broadcast_to(inner, (cat, 128)))[:8]
    for d in range(1, users):
        u2 = lax.rem(u + d, users)
        start(remote(chunks.at[u2], got.at[u], sc.at[d - 1], rc.at[d - 1], u2, i))
        start(remote(inner_out, inner_got.at[u], si.at[d - 1], ri.at[d - 1], u2, i))
    mine.wait()
    for d in range(1, users):
        u2 = lax.rem(u + users - d, users)
        remote(lf.at[u2], lf.at[u2], sl.at[d - 1], rl.at[d - 1], u2, i).wait_recv()
        remote(arrived.at[u2], arrived.at[u2], sd.at[d - 1], rd.at[d - 1], u2, i).wait_recv()
    worker_rows = layer_out.shape[0]
    laid = jnp.zeros((worker_rows, width), f32)
    for v in range(0, users, 2):
        k = col_iota((worker_rows, 2 * slot))
        second = k >= slot
        k = k - jnp.where(second, slot, 0)
        begin = jnp.where(second, lf[v + 1][:1, : 2 * slot], lf[v][:1, : 2 * slot])
        sent_len = jnp.where(second, lf[v + 1][8:9, : 2 * slot], lf[v][8:9, : 2 * slot])
        place = ((k + begin == row_iota((worker_rows, 2 * slot))) & (k < sent_len)).astype(bf16)
        laid = laid + dot_f32(place, arrived[v : v + 2].reshape(2 * slot, width), PLAIN)
    layer_out[...] = laid.astype(bf16)
    total = chunks[u].astype(f32)
    inner_total = inner_out[...]
    for d in range(1, users):
        u2 = lax.rem(u + users - d, users)
        remote(got.at[u2], got.at[u2], sc.at[d - 1], rc.at[d - 1], u2, i).wait_recv()
        remote(inner_got.at[u2], inner_got.at[u2], si.at[d - 1], ri.at[d - 1], u2, i).wait_recv()
        total = total + got[u2].astype(f32)
        inner_total = inner_total + inner_got[u2]
    inner_rows = jnp.transpose(jnp.broadcast_to(inner_total[:1], (128, cat)))
    here = hat[:, pl.ds(pl.multiple_of(u * cols, cols), cols)]
    item_grad[...] = (total - here * inner_rows[:, :cols]) * scale[...]
    for c in sent:
        c.wait_send()


def fused(
    users, items,
    tokens, lengths, destination, worker_offset, positives, negatives, table,
    in_gain, w_uvqk, out_gain, w_out,
):
    f32, bf16 = jnp.float32, jnp.bfloat16
    dma = pltpu.SemaphoreType.DMA
    half = users // 2
    count, width = tokens.shape
    slot = count // lengths.shape[1]
    share = negatives.shape[1] // items
    cat = table.shape[0]
    cols = width // users
    total = w_uvqk.shape[1]
    hd = out_gain.shape[0]
    w3 = w_uvqk.reshape(users, w_uvqk.shape[0] // users, total)
    o3 = w_out.reshape(users, w_out.shape[0] // users, w_out.shape[1])
    smem = pl.BlockSpec(memory_space=pltpu.SMEM)
    any_spec = pl.BlockSpec(memory_space=pl.ANY)
    return pl.pallas_call(
        functools.partial(fused_kernel, users, items),
        out_shape=(
            jax.ShapeDtypeStruct((TOK_DEV, width), bf16),
            jax.ShapeDtypeStruct((count, width), bf16),
            jax.ShapeDtypeStruct((cat, cols), f32),
        ),
        in_specs=[smem] * 3 + [VMEM_SPEC] * 5 + [any_spec, VMEM_SPEC, any_spec],
        out_specs=(VMEM_SPEC,) * 3,
        scratch_shapes=[
            pltpu.VMEM((items,) + w3.shape, bf16),
            pltpu.VMEM((items,) + o3.shape, bf16),
            pltpu.VMEM((items, share, width), bf16),
            pltpu.VMEM((users, 16, 128), jnp.int32),
            pltpu.VMEM((items, share, width), bf16),
            pltpu.VMEM((users, 16, 128), jnp.int32),
            pltpu.VMEM((cat, width), f32),
            pltpu.VMEM((cat, width), bf16),
            pltpu.VMEM((cat, 1), f32),
            pltpu.VMEM((count, width), bf16),
            pltpu.VMEM((count // TILE, TILE, 2 * TILE), f32),
            pltpu.VMEM((count, width), bf16),
            pltpu.VMEM((cat, count), bf16),
            pltpu.VMEM((count, total), f32),
            pltpu.VMEM((count, total), bf16),
            pltpu.VMEM((count, hd), f32),
            pltpu.VMEM((count, width), bf16),
            pltpu.VMEM((users, slot, width), bf16),
            pltpu.VMEM((users, slot, width), bf16),
            pltpu.VMEM((count, width), bf16),
            pltpu.VMEM((count, width), bf16),
            pltpu.VMEM((count, width), bf16),
            pltpu.VMEM((count, items * share), bf16),
            pltpu.VMEM((items, share, width), bf16),
            pltpu.VMEM((items, share, width), bf16),
            pltpu.VMEM((cat, width), f32),
            pltpu.VMEM((users, cat, cols), bf16),
            pltpu.VMEM((users, cat, cols), bf16),
            pltpu.VMEM((8, cat), f32),
            pltpu.VMEM((users, 8, cat), f32),
            pltpu.VMEM((count, 128), f32),
            dma((6,)),
            dma((2, items - 1)), dma((2, items - 1)),
            dma((2, items - 1, 2)), dma((2, items - 1, 2)),
            dma((2, items - 1, half)), dma((2, items - 1, half)),
            dma((2, items - 1, 2)), dma((2, items - 1, 2)),
            dma((items - 1,)), dma((items - 1,)),
            dma((users - 1,)), dma((users - 1,)),
            dma((users - 1,)), dma((users - 1,)),
            dma((items - 1,)), dma((items - 1,)),
            dma((users - 1,)), dma((users - 1,)),
            dma((users - 1,)), dma((users - 1,)),
        ],
        compiler_params=pltpu.CompilerParams(
            collective_id=0, has_side_effects=True, vmem_limit_bytes=60 << 20
        ),
    )(
        lengths, destination, worker_offset, tokens, positives.reshape(1, -1), negatives, table,
        in_gain.reshape(1, -1), w3, out_gain.reshape(1, -1), o3,
    )


def step(users, items, tokens, lengths, destination, worker_offset, positives, negatives, table,
         in_gain, w_uvqk, out_gain, w_out):
    aligned = (
        users % 2 == 0
        and users == 8
        and tokens.shape[0] % TILE == 0
        and tokens.shape[0] // lengths.shape[1] <= TILE // 2
        and table.shape[0] % 256 == 0
        and items > 1
        and w_uvqk.shape[0] % (32 * users) == 0
        and w_out.shape[0] % (32 * users) == 0
        and w_out.shape[1] % 128 == 0
        and tokens.shape[1] == 128 * users
        and table.shape[0] % 128 == 0
        and negatives.shape[1] % (16 * items) == 0
    )
    run = functools.partial(fused, users, items) if aligned else per_device
    return run(tokens, lengths, destination, worker_offset, positives, negatives, table,
               in_gain, w_uvqk, out_gain, w_out)


def solution(mesh):
    return jax.shard_map(
        functools.partial(step, mesh.shape["user"], mesh.shape["item"]),
        mesh=mesh,
        in_specs=(
            P(("user", "item"), None),
            P(("user", "item"), None),
            P(("user", "item"), None),
            P(("user", "item"), None),
            P(("user", "item")),
            P(),
            P("item", None),
            P(),
            P("item", None),
            P(),
            P(None, "item"),
        ),
        out_specs=(P(("user", "item"), None), P(("user", "item"), None), P("item", "user")),
        check_vma=False,
    )
```

```python
import functools

import jax
import jax.numpy as jnp
from jax import lax
from jax.experimental import pallas as pl
from jax.experimental.pallas import tpu as pltpu
from jax.sharding import PartitionSpec as P

HEAD = 128
TOK_DEV = 256


norm_epsilon = 1e-05
scale_epsilon = 1e-06
inverse_temp = 20.0
loss_scale = 32.0


def layer_norm(values, gain):
    center = jnp.mean(values, axis=-1, keepdims=True)
    shifted = values - center
    spread = jnp.mean(shifted * shifted, axis=-1, keepdims=True)
    return shifted * lax.rsqrt(spread + norm_epsilon) * gain


def hstu_block(rows, segment, in_gain, w_uvqk, out_gain, w_out):
    count = rows.shape[0]
    rows_f = rows.astype(jnp.float32)
    normed = layer_norm(rows_f, in_gain).astype(jnp.bfloat16)
    projected = jnp.dot(
        normed,
        lax.all_gather(w_uvqk, "item", axis=0, tiled=True),
        preferred_element_type=jnp.float32,
    )
    active = jax.nn.silu(projected).astype(jnp.bfloat16)
    width = active.shape[1] // 4
    heads = width // HEAD
    gate_u = active[:, :width]
    values_v = active[:, width : 2 * width].reshape(count, heads, HEAD)
    queries = active[:, 2 * width : 3 * width].reshape(count, heads, HEAD)
    key_rows = active[:, 3 * width :].reshape(count, heads, HEAD)
    scores = jnp.einsum(
        "qhd,khd->hqk", queries, key_rows, preferred_element_type=jnp.float32
    ) * HEAD ** (-0.5)
    order = jnp.arange(count, dtype=jnp.int32)
    allowed = (segment[:, None] == segment[None, :]) & (order[None, :] <= order[:, None])
    weights = jnp.where(allowed[None], jax.nn.silu(scores), 0.0).astype(jnp.bfloat16)
    mixed = jnp.einsum(
        "hqk,khd->qhd", weights, values_v, preferred_element_type=jnp.float32
    ).reshape(count, width)
    gated = (layer_norm(mixed, out_gain) * gate_u.astype(jnp.float32)).astype(jnp.bfloat16)
    delta = jnp.dot(
        gated, lax.all_gather(w_out, "item", axis=1, tiled=True), preferred_element_type=jnp.float32
    )
    return (rows_f + delta).astype(jnp.bfloat16)


def dispatch(rows, home_start, history_len, targets, offsets, slot_rows, user_count):
    peers = jnp.arange(user_count, dtype=jnp.int32)
    chosen = (targets[None, :] == peers[:, None]).astype(jnp.int32)
    first_row = jnp.sum(chosen * home_start[None, :], axis=1)
    sent_count = jnp.sum(chosen * history_len[None, :], axis=1)
    landing = jnp.sum(chosen * offsets[None, :], axis=1)
    within = jnp.arange(slot_rows, dtype=jnp.int32)
    picked = jnp.minimum(first_row[:, None] + within[None, :], rows.shape[0] - 1)
    filled = within[None, :] < sent_count[:, None]
    parcels = jnp.where(filled[:, :, None], rows[picked], jnp.zeros((), rows.dtype))
    labels = jnp.stack([landing, sent_count], axis=1)
    arrived, arrived_labels = (
        lax.all_to_all(parcels, "user", split_axis=0, concat_axis=0, tiled=True),
        lax.all_to_all(labels, "user", split_axis=0, concat_axis=0, tiled=True),
    )
    worker_rows = jnp.arange(TOK_DEV, dtype=jnp.int32)
    lower = arrived_labels[:, 0]
    upper = lower + arrived_labels[:, 1]
    inside = (
        (worker_rows[:, None] >= lower[None, :]) & (worker_rows[:, None] < upper[None, :])
    ).astype(jnp.int32)
    source = jnp.sum(inside * peers[None, :], axis=1)
    begin = jnp.sum(inside * lower[None, :], axis=1)
    flattened = arrived.reshape(-1, arrived.shape[-1])
    gathered = flattened[source * slot_rows + worker_rows - begin]
    return (gathered, source, arrived_labels)


def per_device(
    tokens,
    lengths,
    destination,
    worker_offset,
    positives,
    negatives,
    table,
    in_gain,
    w_uvqk,
    out_gain,
    w_out,
):
    user_count = lax.axis_size("user")
    item_count = lax.axis_size("item")
    item_here = lax.axis_index("item")
    user_here = lax.axis_index("user")
    home_rows = tokens.shape[0]
    model_width = tokens.shape[1]
    hist_count = lengths.shape[1]
    slot_rows = home_rows // hist_count
    history_len = lengths[0]
    targets = destination[0]
    offsets = worker_offset[0]
    home_start = jnp.cumsum(history_len) - history_len
    row_ids = jnp.arange(home_rows, dtype=jnp.int32)
    finished = (row_ids[:, None] >= (home_start + history_len)[None, :]).astype(jnp.int32)
    home_segment = jnp.sum(finished, axis=1)
    valid = row_ids < jnp.sum(history_len)
    home_out = hstu_block(tokens, home_segment, in_gain, w_uvqk, out_gain, w_out)
    layer_out = dispatch(
        home_out, home_start, history_len, targets, offsets, slot_rows, user_count
    )[0]
    item_rows = table.shape[0]
    table_f = table.astype(jnp.float32)
    table_scale = lax.rsqrt(jnp.mean(table_f * table_f, axis=1) + scale_epsilon)
    table_hat = table_f * table_scale[:, None]
    table_low = table_hat.astype(jnp.bfloat16)
    share = negatives.shape[1] // item_count
    owned_ids = (
        lax.dynamic_slice_in_dim(negatives, item_here * share, share, 1) - item_here * item_rows
    )
    group_rows = lax.all_to_all(
        table_low[owned_ids], "item", split_axis=0, concat_axis=0, tiled=True
    ).reshape(-1, model_width)
    positive_local = positives - item_here * item_rows
    positive_rows = table_low[positive_local]
    out_f = home_out.astype(jnp.float32)
    out_scale = lax.rsqrt(jnp.mean(out_f * out_f, axis=1) + scale_epsilon)
    out_hat = out_f * out_scale[:, None]
    out_low = out_hat.astype(jnp.bfloat16)
    factor = inverse_temp / model_width
    positive_logit = (
        jnp.einsum("rd,rd->r", out_low, positive_rows, preferred_element_type=jnp.float32) * factor
    )
    negative_logit = (
        jnp.einsum("rd,nd->rn", out_low, group_rows, preferred_element_type=jnp.float32) * factor
    )
    positive_exp = jnp.exp(positive_logit)
    negative_exp = jnp.exp(negative_logit)
    partition = positive_exp + jnp.sum(negative_exp, axis=1)
    weight = jnp.where(valid, loss_scale, 0.0)
    positive_grad = weight * (positive_exp / partition - 1.0)
    negative_grad = (weight[:, None] * negative_exp / partition[:, None]).astype(jnp.bfloat16)
    grad_hat = (
        positive_grad[:, None] * positive_rows.astype(jnp.float32)
        + jnp.dot(negative_grad, group_rows, preferred_element_type=jnp.float32)
    ) * factor
    token_grad = (
        (grad_hat - out_hat * jnp.mean(grad_hat * out_hat, axis=1, keepdims=True))
        * out_scale[:, None]
    ).astype(jnp.bfloat16)
    negative_terms = (
        jnp.einsum("rn,rd->nd", negative_grad, out_low, preferred_element_type=jnp.float32) * factor
    )
    owned_terms = lax.all_to_all(
        negative_terms.reshape(item_count, share, model_width).astype(jnp.bfloat16),
        "item",
        split_axis=0,
        concat_axis=0,
        tiled=True,
    ).astype(jnp.float32)
    positive_terms = (positive_grad * factor)[:, None] * out_low.astype(jnp.float32)
    catalog = jnp.arange(item_rows, dtype=jnp.int32)
    positive_hits = (positive_local[None, :] == catalog[:, None]).astype(jnp.float32)
    negative_hits = (owned_ids.reshape(-1)[None, :] == catalog[:, None]).astype(jnp.float32)
    row_sums = jnp.dot(positive_hits, positive_terms, precision=lax.Precision.HIGHEST)
    row_sums = row_sums + jnp.dot(
        negative_hits, owned_terms.reshape(-1, model_width), precision=lax.Precision.HIGHEST
    )
    column_width = model_width // user_count
    totals = lax.psum(row_sums.astype(jnp.bfloat16), "user").astype(jnp.float32)
    inner = jnp.mean(totals * table_hat, axis=1)
    whole = (totals - table_hat * inner[:, None]) * table_scale[:, None]
    item_grad = lax.dynamic_slice_in_dim(whole, user_here * column_width, column_width, 1)
    return (layer_out, token_grad, item_grad)


MESH = pl.DeviceIdType.MESH
VMEM_SPEC = pl.BlockSpec(memory_space=pltpu.VMEM)


def remote(src, dst, send_sem, recv_sem, user, item):
    return pltpu.make_async_remote_copy(
        src_ref=src,
        dst_ref=dst,
        send_sem=send_sem,
        recv_sem=recv_sem,
        device_id=(user, item),
        device_id_type=MESH,
    )


def greet(users, items, u, i):
    barrier = pltpu.get_barrier_semaphore()
    for d in range(1, users):
        pl.semaphore_signal(
            barrier, inc=1, device_id=(lax.rem(u + d, users), i), device_id_type=MESH
        )
    for d in range(1, items):
        pl.semaphore_signal(
            barrier, inc=1, device_id=(u, lax.rem(i + d, items)), device_id_type=MESH
        )
    return barrier


def col_iota(shape):
    return lax.broadcasted_iota(jnp.int32, shape, 1)


def row_iota(shape):
    return lax.broadcasted_iota(jnp.int32, shape, 0)


def dot_f32(x, y, contract):
    return lax.dot_general(x, y, (contract, ((), ())), preferred_element_type=jnp.float32)


ROWS_T = ((0,), (0,))
PLAIN = ((1,), (0,))
COLS_T = ((1,), (1,))
TILE = 128


def fused_kernel(
    users, items,
    lens, dests, offs, tokens, pos, negs, table, in_gain, w_ref, out_gain, o_ref,
    layer_out, token_grad, item_grad,
    wf, of, nf, lf, rows_out, labels, hat, low, scale, normed, allowed, pos_rows, pick_t,
    acc, active, mixed, home, parcels, arrived, out_low, hi, lo, ngrad, terms, owned, sums,
    chunks, got, inner_out, inner_got, kept,
    own_sem, s1, r1, s2, r2, s3, r3, s4, r4, sn, rn, sl, rl, sd, rd, st, rt, sc, rc, si, ri,
):
    f32, bf16 = jnp.float32, jnp.bfloat16
    u = lax.axis_index("user")
    i = lax.axis_index("item")
    half = users // 2

    def flip(v, bit):
        return v + bit - 2 * bit * lax.rem(v // bit, 2)

    sibling, near_x, near_y = flip(u, 1), flip(u, 2), flip(u, 4)
    across = flip(near_x, 4)
    count, width = tokens.shape
    hist = lens.shape[1]
    slot = count // hist
    cat = table.shape[0]
    share = negs.shape[1] // items
    depth = width // items
    shard_cols = o_ref.shape[2]
    hd = active.shape[1] // 4
    cols = width // users
    factor = inverse_temp / width
    barrier = greet(users, items, u, i)

    ends = []
    total_len = jnp.int32(0)
    starts = []
    for h in range(hist):
        starts.append(total_len)
        total_len = total_len + lens[0, h]
        ends.append(total_len)

    def of_user(v, values):
        out = jnp.int32(0)
        for h in range(hist):
            out = out + jnp.where(dests[0, h] == v, values[h], 0)
        return out

    for v in range(users):
        landing = of_user(v, [offs[0, h] for h in range(hist)])
        sent_len = of_user(v, [lens[0, h] for h in range(hist)])
        labels[v] = jnp.where(row_iota((16, 128)) < 8, landing, sent_len)
    t_f = table[...].astype(f32)
    t_s = lax.rsqrt(jnp.mean(t_f * t_f, axis=1, keepdims=True) + scale_epsilon)
    scale[...] = t_s
    hat[...] = t_f * t_s
    low[...] = hat[...].astype(bf16)
    base = i * cat
    owned_ids = []
    for g in range(items):
        mine_ids = negs[g : g + 1, :share]
        for k in range(1, items):
            mine_ids = jnp.where(i == k, negs[g : g + 1, k * share : (k + 1) * share], mine_ids)
        owned_ids.append(mine_ids - base)
    owned_ids = jnp.concatenate(owned_ids, axis=1)
    neg_hits = (row_iota((cat, items * share)) == owned_ids).astype(bf16)
    rows_out[...] = dot_f32(neg_hits, low[...], ROWS_T).astype(bf16).reshape(rows_out.shape)

    pl.semaphore_wait(barrier, users + items - 2)
    pairs = ((w_ref, wf), (o_ref, of))
    sent = []

    def start(c):
        c.start()
        sent.append(c)

    for a, (src, dst) in enumerate(pairs):
        for d in range(1, items):
            start(remote(src.at[u], dst.at[i, u], s1.at[a, d - 1], r1.at[a, d - 1], u, lax.rem(i + d, items)))
    for d in range(1, items):
        i2 = lax.rem(i + d, items)
        start(remote(rows_out.at[i2], nf.at[i], sn.at[d - 1], rn.at[d - 1], u, i2))
    for d in range(1, users):
        u2 = lax.rem(u + d, users)
        start(remote(labels.at[u2], lf.at[u], sl.at[d - 1], rl.at[d - 1], u2, i))
    local = [
        pltpu.make_async_copy(o_ref, of.at[i], own_sem.at[0]),
        pltpu.make_async_copy(rows_out.at[i], nf.at[i], own_sem.at[1]),
        pltpu.make_async_copy(labels.at[u], lf.at[u], own_sem.at[2]),
        pltpu.make_async_copy(w_ref, wf.at[i], own_sem.at[5]),
    ]
    for c in local:
        c.start()

    def place_of(a, d, v):
        return pairs[a][1].at[lax.rem(i + items - d, items), v]

    def halves(a, d, v):
        rows = pairs[a][1].shape[2]
        i2 = lax.rem(i + items - d, items)
        return [pairs[a][1].at[i2, v, : rows // 2], pairs[a][1].at[i2, v, rows // 2 :]]

    def move(piece, ss, rr, a, d, e, v):
        return remote(piece, piece, ss.at[a, d - 1, e], rr.at[a, d - 1, e], v, i)

    def first_hop(a, d):
        piece = place_of(a, d, u)
        i2 = lax.rem(i + items - d, items)
        remote(piece, piece, s1.at[a, d - 1], r1.at[a, d - 1], u, i2).wait_recv()
        start(move(piece, s2, r2, a, d, 0, near_x))
        start(move(piece, s2, r2, a, d, 1, near_y))
        start(move(piece, s3, r3, a, d, 0, sibling))

    def second_hop(a, d):
        piece = place_of(a, d, near_x)
        move(piece, s2, r2, a, d, 0, near_x).wait_recv()
        start(move(halves(a, d, near_x)[0], s4, r4, a, d, 0, near_y))
        start(move(piece, s3, r3, a, d, 1, sibling))
        piece = place_of(a, d, near_y)
        move(piece, s2, r2, a, d, 1, near_y).wait_recv()
        start(move(halves(a, d, near_y)[1], s4, r4, a, d, 1, near_x))
        start(move(piece, s3, r3, a, d, 2, sibling))

    def third_hop(a, d):
        first, second = halves(a, d, across)
        move(first, s4, r4, a, d, 0, near_y).wait_recv()
        move(second, s4, r4, a, d, 1, near_x).wait_recv()
        start(move(place_of(a, d, across), s3, r3, a, d, 3, sibling))

    def last_hop(a, d):
        for e, v in enumerate((sibling, flip(sibling, 2), flip(sibling, 4), flip(flip(sibling, 2), 4))):
            move(place_of(a, d, v), s3, r3, a, d, e, sibling).wait_recv()

    @pl.loop(0, count // TILE)
    def _(t):
        rs = pl.ds(pl.multiple_of(t * TILE, TILE), TILE)
        normed[rs, :] = layer_norm(tokens[rs, :].astype(f32), in_gain[...]).astype(bf16)

    wide = 256

    def project(d):
        i2 = lax.rem(i + items - d, items)
        x_cols = pl.ds(pl.multiple_of(i2 * depth, depth), depth)

        @pl.loop(0, active.shape[1] // wide)
        def _(t):
            cs = pl.ds(pl.multiple_of(t * wide, wide), wide)
            block = wf[i2, :, :, cs].reshape(depth, wide)
            part = dot_f32(normed[:, x_cols], block, PLAIN)
            if d == 0:
                acc[:, cs] = part
            elif d < items - 1:
                acc[:, cs] = acc[:, cs] + part
            else:
                active[:, cs] = jax.nn.silu(acc[:, cs] + part).astype(bf16)

    def prepare_mask():
        @pl.loop(0, count // TILE)
        def _(t):
            rows = row_iota((TILE, 2 * TILE)) + t * TILE
            keys = col_iota((TILE, 2 * TILE)) + (t - 1) * TILE
            row_seg = jnp.zeros_like(rows)
            key_seg = jnp.zeros_like(rows)
            for h in range(hist):
                row_seg = row_seg + (rows >= ends[h]).astype(jnp.int32)
                key_seg = key_seg + (keys >= ends[h]).astype(jnp.int32)
            ok = (row_seg == key_seg) & (keys <= rows) & (keys >= 0)
            allowed[t] = ok.astype(f32)

    def prepare_positives():
        pick_t[...] = (row_iota((cat, count)) == pos[...] - base).astype(bf16)

        @pl.loop(0, count // TILE)
        def _(t):
            rs = pl.ds(pl.multiple_of(t * TILE, TILE), TILE)
            pos_rows[rs, :] = dot_f32(pick_t[:, rs], low[...], ROWS_T).astype(bf16)

    steps = range(1, items)
    local[3].wait()
    project(0)
    for d in steps:
        first_hop(0, d)
        if d == 1:
            prepare_positives()
            prepare_mask()
        else:
            second_hop(0, d - 1)
    first_hop(1, 1)
    third_hop(0, 1)
    second_hop(0, items - 1)
    for d in steps:
        if d > 1:
            first_hop(1, d)
            third_hop(0, d)
        if d == items - 1:
            for k in steps:
                second_hop(1, k)
        last_hop(0, d)
        project(d)
    for d in steps:
        third_hop(1, d)

    @pl.loop(0, hd // HEAD)
    def _(h):
        def part_of(k):
            return pl.ds(pl.multiple_of(k * hd + h * HEAD, HEAD), HEAD)

        for t in range(count // TILE):
            first = max(t - 1, 0) * TILE
            keys = slice(first, (t + 1) * TILE)
            rows = slice(t * TILE, (t + 1) * TILE)
            s = dot_f32(active[rows, part_of(2)], active[keys, part_of(3)], COLS_T) * HEAD ** (-0.5)
            mask = allowed[t][:, 2 * TILE - s.shape[1] :]
            wgt = jnp.where(mask > 0.5, jax.nn.silu(s), 0.0).astype(bf16)
            mixed[rows, pl.ds(pl.multiple_of(h * HEAD, HEAD), HEAD)] = dot_f32(
                wgt, active[keys, part_of(1)], PLAIN
            )

    for c in local[:3]:
        c.wait()
    for d in range(1, items):
        last_hop(1, d)

    @pl.loop(0, count // TILE)
    def _(t):
        rs = pl.ds(pl.multiple_of(t * TILE, TILE), TILE)
        gated = (layer_norm(mixed[rs, :], out_gain[...]) * active[rs, :hd].astype(f32)).astype(bf16)
        for k in range(items):
            cs = slice(k * shard_cols, (k + 1) * shard_cols)
            delta = dot_f32(gated, of[k].reshape(hd, shard_cols), PLAIN)
            home[rs, cs] = (tokens[rs, cs].astype(f32) + delta).astype(bf16)

    for d in range(1, items):
        i2 = lax.rem(i + items - d, items)
        remote(nf.at[i2], nf.at[i2], sn.at[d - 1], rn.at[d - 1], u, i2).wait_recv()

    @pl.loop(0, count // TILE)
    def _(t):
        rs = pl.ds(pl.multiple_of(t * TILE, TILE), TILE)
        group = nf[...].reshape(items * share, width)
        out_f = home[rs, :].astype(f32)
        out_scale = lax.rsqrt(jnp.mean(out_f * out_f, axis=1, keepdims=True) + scale_epsilon)
        o_low = (out_f * out_scale).astype(bf16)
        out_low[rs, :] = o_low
        pos_logit = (
            jnp.sum(o_low.astype(f32) * pos_rows[rs, :].astype(f32), axis=1, keepdims=True) * factor
        )
        neg_exp = jnp.exp(dot_f32(o_low, group, COLS_T) * factor)
        pos_exp = jnp.exp(pos_logit)
        partition = pos_exp + jnp.sum(neg_exp, axis=1, keepdims=True)
        ids = row_iota((TILE, 1)) + t * TILE
        weight = jnp.where(ids < total_len, loss_scale, 0.0)
        pos_grad = weight * (pos_exp / partition - 1.0)
        ngrad[rs, :] = (weight * neg_exp / partition).astype(bf16)
        kept[rs, :] = jnp.where(col_iota((TILE, 128)) == 0, pos_grad, out_scale)

    terms[...] = (dot_f32(ngrad[...], out_low[...], ROWS_T) * factor).astype(bf16).reshape(terms.shape)
    for d in range(1, items):
        i2 = lax.rem(i + d, items)
        start(remote(terms.at[i2], owned.at[i], st.at[d - 1], rt.at[d - 1], u, i2))
    own = pltpu.make_async_copy(terms.at[i], owned.at[i], own_sem.at[4])
    own.start()

    @pl.loop(0, users)
    def _(v):
        begin = of_user(v, starts)
        sent_len = of_user(v, [lens[0, h] for h in range(hist)])
        k = row_iota((slot, count))
        pick = ((k + begin == col_iota((slot, count))) & (k < sent_len)).astype(bf16)
        parcels[v] = dot_f32(pick, home[...], PLAIN).astype(bf16)

    for d in range(1, users):
        u2 = lax.rem(u + d, users)
        start(remote(parcels.at[u2], arrived.at[u], sd.at[d - 1], rd.at[d - 1], u2, i))
    mine = pltpu.make_async_copy(parcels.at[u], arrived.at[u], own_sem.at[3])
    mine.start()

    @pl.loop(0, count // TILE)
    def _(t):
        rs = pl.ds(pl.multiple_of(t * TILE, TILE), TILE)
        group = nf[...].reshape(items * share, width)
        pos_grad = kept[rs, :1]
        out_scale = kept[rs, 1:2]
        pos_terms = (pos_grad * factor) * out_low[rs, :].astype(f32)
        top = pos_terms.astype(bf16)
        hi[rs, :] = top
        lo[rs, :] = (pos_terms - top.astype(f32)).astype(bf16)
        out_hat = home[rs, :].astype(f32) * out_scale
        grad_hat = (
            pos_grad * pos_rows[rs, :].astype(f32) + dot_f32(ngrad[rs, :], group, PLAIN)
        ) * factor
        inner = jnp.mean(grad_hat * out_hat, axis=1, keepdims=True)
        token_grad[rs, :] = ((grad_hat - out_hat * inner) * out_scale).astype(bf16)

    sums[...] = dot_f32(pick_t[...], hi[...], PLAIN) + dot_f32(pick_t[...], lo[...], PLAIN)
    hits = (row_iota((cat, items * share)) == owned_ids).astype(bf16)
    own.wait()
    for d in range(1, items):
        i2 = lax.rem(i + items - d, items)
        remote(owned.at[i2], owned.at[i2], st.at[d - 1], rt.at[d - 1], u, i2).wait_recv()
    row_sums = sums[...] + dot_f32(hits, owned[...].reshape(items * share, width), PLAIN)
    for v in range(users):
        chunks[v] = row_sums[:, v * cols : (v + 1) * cols].astype(bf16)
    for d in range(1, users):
        u2 = lax.rem(u + d, users)
        start(remote(chunks.at[u2], got.at[u], sc.at[d - 1], rc.at[d - 1], u2, i))
    inner = jnp.mean(row_sums * hat[...], axis=1, keepdims=True)
    inner_out[...] = jnp.transpose(jnp.broadcast_to(inner, (cat, 128)))[:8]
    for d in range(1, users):
        u2 = lax.rem(u + d, users)
        start(remote(inner_out, inner_got.at[u], si.at[d - 1], ri.at[d - 1], u2, i))
    mine.wait()
    for d in range(1, users):
        u2 = lax.rem(u + users - d, users)
        remote(lf.at[u2], lf.at[u2], sl.at[d - 1], rl.at[d - 1], u2, i).wait_recv()
        remote(arrived.at[u2], arrived.at[u2], sd.at[d - 1], rd.at[d - 1], u2, i).wait_recv()
    worker_rows = layer_out.shape[0]
    laid = jnp.zeros((worker_rows, width), f32)
    for v in range(0, users, 2):
        k = col_iota((worker_rows, 2 * slot))
        second = k >= slot
        k = k - jnp.where(second, slot, 0)
        begin = jnp.where(second, lf[v + 1][:1, : 2 * slot], lf[v][:1, : 2 * slot])
        sent_len = jnp.where(second, lf[v + 1][8:9, : 2 * slot], lf[v][8:9, : 2 * slot])
        place = ((k + begin == row_iota((worker_rows, 2 * slot))) & (k < sent_len)).astype(bf16)
        laid = laid + dot_f32(place, arrived[v : v + 2].reshape(2 * slot, width), PLAIN)
    layer_out[...] = laid.astype(bf16)
    total = chunks[u].astype(f32)
    inner_total = inner_out[...]
    for d in range(1, users):
        u2 = lax.rem(u + users - d, users)
        remote(got.at[u2], got.at[u2], sc.at[d - 1], rc.at[d - 1], u2, i).wait_recv()
        remote(inner_got.at[u2], inner_got.at[u2], si.at[d - 1], ri.at[d - 1], u2, i).wait_recv()
        total = total + got[u2].astype(f32)
        inner_total = inner_total + inner_got[u2]
    inner_rows = jnp.transpose(jnp.broadcast_to(inner_total[:1], (128, cat)))
    here = hat[:, pl.ds(pl.multiple_of(u * cols, cols), cols)]
    item_grad[...] = (total - here * inner_rows[:, :cols]) * scale[...]
    for c in sent:
        c.wait_send()


def fused(
    users, items,
    tokens, lengths, destination, worker_offset, positives, negatives, table,
    in_gain, w_uvqk, out_gain, w_out,
):
    f32, bf16 = jnp.float32, jnp.bfloat16
    dma = pltpu.SemaphoreType.DMA
    half = users // 2
    count, width = tokens.shape
    slot = count // lengths.shape[1]
    share = negatives.shape[1] // items
    cat = table.shape[0]
    cols = width // users
    total = w_uvqk.shape[1]
    hd = out_gain.shape[0]
    w3 = w_uvqk.reshape(users, w_uvqk.shape[0] // users, total)
    o3 = w_out.reshape(users, w_out.shape[0] // users, w_out.shape[1])
    smem = pl.BlockSpec(memory_space=pltpu.SMEM)
    any_spec = pl.BlockSpec(memory_space=pl.ANY)
    return pl.pallas_call(
        functools.partial(fused_kernel, users, items),
        out_shape=(
            jax.ShapeDtypeStruct((TOK_DEV, width), bf16),
            jax.ShapeDtypeStruct((count, width), bf16),
            jax.ShapeDtypeStruct((cat, cols), f32),
        ),
        in_specs=[smem] * 3 + [VMEM_SPEC] * 5 + [any_spec, VMEM_SPEC, any_spec],
        out_specs=(VMEM_SPEC,) * 3,
        scratch_shapes=[
            pltpu.VMEM((items,) + w3.shape, bf16),
            pltpu.VMEM((items,) + o3.shape, bf16),
            pltpu.VMEM((items, share, width), bf16),
            pltpu.VMEM((users, 16, 128), jnp.int32),
            pltpu.VMEM((items, share, width), bf16),
            pltpu.VMEM((users, 16, 128), jnp.int32),
            pltpu.VMEM((cat, width), f32),
            pltpu.VMEM((cat, width), bf16),
            pltpu.VMEM((cat, 1), f32),
            pltpu.VMEM((count, width), bf16),
            pltpu.VMEM((count // TILE, TILE, 2 * TILE), f32),
            pltpu.VMEM((count, width), bf16),
            pltpu.VMEM((cat, count), bf16),
            pltpu.VMEM((count, total), f32),
            pltpu.VMEM((count, total), bf16),
            pltpu.VMEM((count, hd), f32),
            pltpu.VMEM((count, width), bf16),
            pltpu.VMEM((users, slot, width), bf16),
            pltpu.VMEM((users, slot, width), bf16),
            pltpu.VMEM((count, width), bf16),
            pltpu.VMEM((count, width), bf16),
            pltpu.VMEM((count, width), bf16),
            pltpu.VMEM((count, items * share), bf16),
            pltpu.VMEM((items, share, width), bf16),
            pltpu.VMEM((items, share, width), bf16),
            pltpu.VMEM((cat, width), f32),
            pltpu.VMEM((users, cat, cols), bf16),
            pltpu.VMEM((users, cat, cols), bf16),
            pltpu.VMEM((8, cat), f32),
            pltpu.VMEM((users, 8, cat), f32),
            pltpu.VMEM((count, 128), f32),
            dma((6,)),
            dma((2, items - 1)), dma((2, items - 1)),
            dma((2, items - 1, 2)), dma((2, items - 1, 2)),
            dma((2, items - 1, half)), dma((2, items - 1, half)),
            dma((2, items - 1, 2)), dma((2, items - 1, 2)),
            dma((items - 1,)), dma((items - 1,)),
            dma((users - 1,)), dma((users - 1,)),
            dma((users - 1,)), dma((users - 1,)),
            dma((items - 1,)), dma((items - 1,)),
            dma((users - 1,)), dma((users - 1,)),
            dma((users - 1,)), dma((users - 1,)),
        ],
        compiler_params=pltpu.CompilerParams(
            collective_id=0, has_side_effects=True, vmem_limit_bytes=60 << 20
        ),
    )(
        lengths, destination, worker_offset, tokens, positives.reshape(1, -1), negatives, table,
        in_gain.reshape(1, -1), w3, out_gain.reshape(1, -1), o3,
    )


def step(users, items, tokens, lengths, destination, worker_offset, positives, negatives, table,
         in_gain, w_uvqk, out_gain, w_out):
    aligned = (
        users % 2 == 0
        and users == 8
        and tokens.shape[0] % TILE == 0
        and tokens.shape[0] // lengths.shape[1] <= TILE // 2
        and table.shape[0] % 256 == 0
        and items > 1
        and w_uvqk.shape[0] % (32 * users) == 0
        and w_out.shape[0] % (32 * users) == 0
        and w_out.shape[1] % 128 == 0
        and tokens.shape[1] == 128 * users
        and table.shape[0] % 128 == 0
        and negatives.shape[1] % (16 * items) == 0
    )
    run = functools.partial(fused, users, items) if aligned else per_device
    return run(tokens, lengths, destination, worker_offset, positives, negatives, table,
               in_gain, w_uvqk, out_gain, w_out)


def solution(mesh):
    return jax.shard_map(
        functools.partial(step, mesh.shape["user"], mesh.shape["item"]),
        mesh=mesh,
        in_specs=(
            P(("user", "item"), None),
            P(("user", "item"), None),
            P(("user", "item"), None),
            P(("user", "item"), None),
            P(("user", "item")),
            P(),
            P("item", None),
            P(),
            P("item", None),
            P(),
            P(None, "item"),
        ),
        out_specs=(P(("user", "item"), None), P(("user", "item"), None), P("item", "user")),
        check_vma=False,
    )
```
